512 devices in a mesh: row: 16 (over x, y_lo), col: 32 (over y_hi, z, core).
Axes of the slice: x: 4, y: 8 (y_hi: 2, y_lo: 4; y = y_hi * 4 + y_lo), z: 8, core: 2. Of those that a mesh axis runs over, the one named last changes fastest.
Arguments:
- bricks: bfloat16 [16, 32, 2, 16, 128, 128], P('row', 'col'), may hold values from -393216 to 393216
- brick_coords: int32 [16, 32, 3, 2], P('row', 'col'), may hold values from 0 to 31, as said below
- brick_counts: int32 [16, 32], P('row', 'col'), may hold values from 0 to 2, as said below
- step_sizes: float32 [2, 3], replicated, may hold values from 0.3 to 1
- init_a: float32 [16, 512, 256], P('row', 'col'), may hold values from -6 to 6
- init_b: float32 [32, 256, 256], P('col', 'row'), may hold values from -6 to 6
- init_c: float32 [512, 256], replicated, may hold values from -6 to 6
Outputs:
- factor_a: float32 [16, 512, 256], P('row', 'col')
- factor_b: float32 [32, 256, 256], P('col', 'row')
- factor_c: float32 [512, 256], replicated
The draws below stay inside these ranges and needn't reach their ends.
Inputs may be any that keep to these rules, and one draw needn't show every extreme that they name: brick_counts of rows r and (r + half of the row axis) mod the row axis in one column add up to at most 3; some device holds 2 bricks. `brick_coords`: component 0 is below 4, component 1 below 2, component 2 below 32; dead slots hold arbitrary positions.
All inputs are finite; a program needn't handle non-finite values.
Results may differ from the reference program's by a relative error of at most 0.0003.
The reference program's roundings to bfloat16 on the way count: a program that leaves them out, or rounds other values in their place, can miss the bound.
Values may be sent and summed in bfloat16 or wider, within the bound.
No kernel may reach another device: no remote copies, remote signals or barrier semaphores. Data moves between devices by JAX's collectives and lax.ppermute only.
A program may use at most 64 MiB of HBM per device.

```python
import math
import jax
import jax.numpy as jnp
from jax import lax

R = 256
TILE = 128
BK = 16
TI = 4
TJ = 2
KT = 32
MAXB = 2
SWEEPS = 2
J = 8192
K = 512
N_ROW = 16
N_COL = 32


def draw_brick_counts(key, part):
    half = N_ROW // 2
    keys = jax.random.split(key, 5)
    total = jax.random.randint(keys[0], (half, N_COL), 0, MAXB + 2)
    forced_row = jax.random.randint(keys[1], (), 0, half)
    forced_col = jax.random.randint(keys[2], (), 0, N_COL)
    hit = (jnp.arange(half)[:, None] == forced_row) & (jnp.arange(N_COL)[None, :] == forced_col)
    total = jnp.where(hit, MAXB + 1, total)
    low = jnp.maximum(total - MAXB, 0)
    high = jnp.minimum(total, MAXB)
    first = jax.random.randint(keys[3], (half, N_COL), low, high + 1)
    first = jnp.where(hit, MAXB, first)
    second = total - first
    flip = jax.random.randint(keys[4], (half, N_COL), 0, 2)
    upper = jnp.where(flip == 1, first, second)
    lower = total - upper
    return jnp.concatenate([upper, lower], axis=0).astype(jnp.int32)


def draw_brick_coords(key, part):
    keys = jax.random.split(key, 3)
    shape = (N_ROW, N_COL, 1, MAXB)
    first = jax.random.randint(keys[0], shape, 0, TI)
    second = jax.random.randint(keys[1], shape, 0, TJ)
    third = jax.random.randint(keys[2], shape, 0, KT)
    return jnp.concatenate([first, second, third], axis=2).astype(jnp.int32)


def shard_levels(own_key, dims, shards, least, top_value):
    gain, own = 1.0, jax.random.fold_in(own_key, 6)
    for axis_at, blocks in shards:
        steps = jnp.exp(jax.random.uniform(jax.random.fold_in(own, axis_at), (blocks,), jnp.float32, least / len(shards), top_value / len(shards)))
        gain = gain * jnp.repeat(steps, dims[axis_at] // blocks).reshape([-1 if axis == axis_at else 1 for axis in range(len(dims))])
    return gain


def noise(rng, extent, scale, most, cuts=(), kind=jnp.bfloat16):
    array = jax.random.normal(rng, extent, jnp.float32) * scale
    if len(cuts) > 0:
        array = shard_levels(rng, extent, cuts, -0.22, 0.18) * array
    return jnp.clip(array, min=-most, max=most).astype(kind)


def setup_inputs(seed: int = 0) -> dict:
    key_list = jax.random.split(jax.random.key(seed), 8)
    return {
        "bricks": noise(key_list[0], (N_ROW, N_COL, MAXB, BK, TILE, TILE), (2 * J * K // TILE), 393216.0, ((0, 16), (1, 32))),
        "brick_coords": draw_brick_coords(jax.random.fold_in(key_list[7], 71), 0),
        "brick_counts": draw_brick_counts(jax.random.fold_in(key_list[7], 71), 0),
        "step_sizes": jnp.clip(jnp.exp(jax.random.uniform(key_list[3], (SWEEPS, 3), jnp.float32, math.log(0.3), math.log(1.0))), 0.3, 1.0),
        "init_a": noise(key_list[4], (N_ROW, TI * TILE, R), 1.0, 6.0, ((0, 16), (1, 32)), jnp.float32),
        "init_b": noise(key_list[5], (N_COL, TJ * TILE, R), 1.0, 6.0, ((0, 32), (1, 16)), jnp.float32),
        "init_c": noise(key_list[6], (K, R), 1.0, 6.0, (), jnp.float32),
    }


def brick_terms(brick, a_tile, b_tile, c_rows):
    block = brick.astype(jnp.float32)
    a_full = a_tile.astype(jnp.float32)
    b_full = b_tile.astype(jnp.float32)
    c_wide = c_rows.astype(jnp.float32)[:, None, :]
    wide = jnp.einsum("kij,jr->kir", block, b_full)
    along_a = jnp.sum(wide * c_wide, axis=0)
    deep = jnp.einsum("kij,ir->kjr", block, a_full)
    along_b = jnp.sum(deep * c_wide, axis=0)
    along_c = jnp.sum(deep * b_full[None, :, :], axis=1)
    return along_a, along_b, along_c


def add_tile(total, delta, start):
    old = lax.dynamic_slice_in_dim(total, start, delta.shape[0], 0)
    return lax.dynamic_update_slice_in_dim(total, old + delta, start, 0)


def gram(values):
    return jnp.dot(values.T, values, preferred_element_type=jnp.float32)


def project(state, hess, drive, rate):
    scale = jnp.sum(jnp.abs(hess), axis=1) + 1e-6
    slope = jnp.dot(state, hess, precision=lax.Precision.HIGHEST, preferred_element_type=jnp.float32) - drive
    return jnp.maximum(state - rate * slope / scale[None, :], 0.0)


def reference(bricks, brick_coords, brick_counts, step_sizes, init_a, init_b, init_c):
    slots = N_ROW * N_COL * MAXB
    flat = bricks.reshape(slots, BK, TILE, TILE)
    spots = jnp.transpose(brick_coords, (0, 1, 3, 2)).reshape(slots, 3).astype(jnp.int32)
    number = jnp.arange(slots, dtype=jnp.int32)
    row_of = number // (N_COL * MAXB)
    col_of = (number // MAXB) % N_COL
    slot_of = number % MAXB
    alive = slot_of < brick_counts.reshape(-1)[number // MAXB]
    i_start = ((row_of * TI + spots[:, 0]) * TILE).astype(jnp.int32)
    j_start = ((col_of * TJ + spots[:, 1]) * TILE).astype(jnp.int32)
    k_start = (spots[:, 2] * BK).astype(jnp.int32)
    state_a = init_a.reshape(N_ROW * TI * TILE, R)
    state_b = init_b.reshape(N_COL * TJ * TILE, R)
    state_c = init_c
    for sweep in range(SWEEPS):
        a_bf = state_a.astype(jnp.bfloat16)
        b_bf = state_b.astype(jnp.bfloat16)
        c_bf = state_c.astype(jnp.bfloat16)

        def visit(carry, item):
            brick, live, i_low, j_low, k_low = item

            def work(inner):
                total_a, total_b, total_c = inner
                a_tile = lax.dynamic_slice_in_dim(a_bf, i_low, TILE, 0)
                b_tile = lax.dynamic_slice_in_dim(b_bf, j_low, TILE, 0)
                c_rows = lax.dynamic_slice_in_dim(c_bf, k_low, BK, 0)
                delta_a, delta_b, delta_c = brick_terms(brick, a_tile, b_tile, c_rows)
                return (add_tile(total_a, delta_a, i_low), add_tile(total_b, delta_b, j_low), add_tile(total_c, delta_c, k_low))

            def skip(inner):
                return inner

            return lax.cond(live, work, skip, carry), None

        start = (jnp.zeros(state_a.shape, jnp.float32), jnp.zeros(state_b.shape, jnp.float32), jnp.zeros(state_c.shape, jnp.float32))
        (drive_a, drive_b, drive_c), _ = lax.scan(visit, start, (flat, alive, i_start, j_start, k_start))
        gram_a = gram(a_bf)
        gram_b = gram(b_bf)
        gram_c = gram(c_bf)
        new_a = project(state_a, gram_b * gram_c, drive_a, step_sizes[sweep, 0])
        new_b = project(state_b, gram_a * gram_c, drive_b, step_sizes[sweep, 1])
        new_c = project(state_c, gram_a * gram_b, drive_c, step_sizes[sweep, 2])
        state_a, state_b, state_c = new_a, new_b, new_c
    return state_a.reshape(N_ROW, TI * TILE, R), state_b.reshape(N_COL, TJ * TILE, R), state_c
```

```python
import jax
import jax.numpy as jnp
from jax import lax
from jax.sharding import PartitionSpec as P

LANES = 128
HIGH = lax.Precision.HIGHEST


def swap(x, axis):
    return lax.all_to_all(x, axis, 0, 0, tiled=True)


def spread(x, peers):
    return lax.optimization_barrier(jnp.broadcast_to(x[None], (peers,) + x.shape))


def pad_lanes(x):
    short = -x.shape[-1] % LANES
    return jnp.pad(x, [(0, 0)] * (x.ndim - 1) + [(0, short)])


def fold(x):
    lead, (m, n) = x.shape[:-2], x.shape[-2:]
    parts = [x[..., t * LANES : (t + 1) * LANES] for t in range(n // LANES)]
    return jnp.concatenate(parts, axis=-2)


def unfold(x, n):
    tiles = n // LANES
    m = x.shape[-2] // tiles
    return jnp.concatenate([x[..., t * m : (t + 1) * m, :] for t in range(tiles)], axis=-1)


def take(x, sizes):
    out, at = [], 0
    for size in sizes:
        out.append(x[:, at : at + size])
        at += size
    return out


def gram(values):
    return sum(
        lax.dot_general(v, v, (((1,), (1,)), ((), ())), preferred_element_type=jnp.float32)
        for v in values
    )


def bump(state, hess, full, drive, rate):
    scale = jnp.sum(jnp.abs(hess), axis=1) + 1e-06
    push = jnp.stack(
        [jnp.dot(hess, f, precision=HIGH, preferred_element_type=jnp.float32) for f in full]
    )
    return jnp.maximum(state - rate * (push - drive) / scale[None, :, None], 0.0)


def brick_terms(brick, a_tile, b_tile, c_rows):
    c_wide = c_rows.astype(jnp.float32)[:, None, :]
    wide = jnp.einsum("kij,qj->kiq", brick, b_tile, preferred_element_type=jnp.float32)
    along_a = jnp.sum(wide * c_wide, axis=0)
    deep = jnp.einsum("kij,qi->kjq", brick, a_tile, preferred_element_type=jnp.float32)
    along_b = jnp.sum(deep * c_wide, axis=0)
    along_c = jnp.sum(deep * b_tile.T.astype(jnp.float32)[None, :, :], axis=1)
    return along_a.T, along_b.T, along_c.T


def shards(bricks, brick_coords, brick_counts, step_sizes, init_a, init_b, init_c):
    nr, nc = lax.axis_size("row"), lax.axis_size("col")
    row, col = lax.axis_index("row"), lax.axis_index("col")
    slab, places, own = bricks[0, 0], brick_coords[0, 0], brick_counts[0, 0]
    slots, depth, tile, _ = slab.shape
    sweeps = step_sizes.shape[0]
    rank = init_a.shape[-1]
    own_a, own_b = init_a.shape[1], init_b.shape[1]
    tiles_a, tiles_b = own_a * nc // tile, own_b * nr // tile
    length = init_c.shape[0]
    layers = length // depth
    qa, qb, ka = rank // nc, rank // nr, length // nr
    f32, bf16 = jnp.float32, jnp.bfloat16
    half = rank // LANES

    live = lax.iota(jnp.int32, slots) < own
    spots = jnp.where(live[None, :], places, 0)
    mine = pad_lanes(jnp.where(live[None, :], places, -1).astype(f32).reshape(1, -1))
    mine = jnp.broadcast_to(mine, (8, LANES))

    state_a, state_b = init_a[0], init_b[0]
    c_bf = init_c.astype(bf16)
    crow_t = lax.dynamic_slice_in_dim(init_c, row * ka, ka, 0).T

    for sweep in range(sweeps):
        first = sweep == 0
        if first:
            got = swap(spread(jnp.concatenate([fold(state_a), mine], 0), nc), "col")
            rows, spots_col = take(got, [own_a * half, 8])
            rows = unfold(rows, rank).reshape(tiles_a, tile, rank)
            at3 = jnp.swapaxes(rows, 1, 2)
            spots_col = spots_col[:, 0, : 3 * slots].reshape(nc, 3, slots).astype(jnp.int32)
        else:
            send = jnp.concatenate([new_a.reshape(-1, LANES), fold(pad_lanes(new_c))], 0)
            got = swap(spread(send, nc), "col")
            chunk, c_got = take(got, [tiles_a * qa, send.shape[0] - tiles_a * qa])
            at3 = jnp.swapaxes(chunk.reshape(nc, tiles_a, qa, tile), 0, 1).reshape(tiles_a, rank, tile)
            crow_t = unfold(c_got, new_c.shape[1] + -new_c.shape[1] % LANES)[:, :, :ka].reshape(rank, ka)
        at3_bf = at3.astype(bf16)
        gram_a = gram(at3_bf)
        slice_a = lax.dynamic_slice_in_dim(gram_a, col * qa, qa, 0)
        if first:
            send = jnp.concatenate([fold(state_b), fold(slice_a)], 0)
            got = swap(spread(send, nr), "row")
            rows, s_got = take(got, [own_b * half, qa * half])
            rows = unfold(rows, rank).reshape(tiles_b, tile, rank)
            bt3 = jnp.swapaxes(rows, 1, 2)
        else:
            send = jnp.concatenate(
                [new_b.reshape(-1, LANES), fold(slice_a), fold(crow_t.T)], 0
            )
            got = swap(spread(send, nr), "row")
            chunk, s_got, c_got = take(got, [tiles_b * qb, qa * half, ka * half])
            bt3 = jnp.swapaxes(chunk.reshape(nr, tiles_b, qb, tile), 0, 1).reshape(tiles_b, rank, tile)
            c_bf = unfold(c_got, rank).reshape(length, rank).astype(bf16)
        bt3_bf = bt3.astype(bf16)
        gram_b = gram(bt3_bf)
        sa_c = unfold(jnp.sum(s_got, axis=0), rank)
        gram_c = lax.dot_general(
            c_bf, c_bf, (((0,), (0,)), ((), ())), preferred_element_type=f32
        )
        parts_a, parts_c = [], []
        drive_b = jnp.zeros((tiles_b, rank, tile), f32)
        for slot in range(slots):
            ti, tj, tk = spots[0, slot], spots[1, slot], spots[2, slot]
            a_tile = lax.dynamic_index_in_dim(at3_bf, ti, 0, keepdims=False)
            b_tile = lax.dynamic_index_in_dim(bt3_bf, tj, 0, keepdims=False)
            c_rows = lax.dynamic_slice_in_dim(c_bf, tk * depth, depth, 0)
            da, db, dc = brick_terms(slab[slot], a_tile, b_tile, c_rows)
            parts_a.append(da)
            parts_c.append(dc)
            here = (lax.iota(jnp.int32, tiles_b) == tj) & live[slot]
            drive_b = drive_b + jnp.where(here[:, None, None], db[None], 0.0)
        pieces = [p.reshape(nc, qa, tile) for p in parts_a]
        pieces.append(fold(gram_b.reshape(nc, qa, rank)))
        pieces.append(pad_lanes(jnp.concatenate(parts_c, axis=1)).reshape(nc, qa, LANES))
        got = swap(jnp.concatenate(pieces, axis=1), "col")
        *a_got, s_got, c_got = take(got, [qa] * slots + [qa * half, qa])
        sb_c = unfold(jnp.sum(s_got, axis=0), rank)
        drive_a = jnp.stack(
            [
                sum(
                    jnp.sum(jnp.where((spots_col[:, 0, m] == t)[:, None, None], a_got[m], 0.0), axis=0)
                    for m in range(slots)
                )
                for t in range(tiles_a)
            ]
        )
        onehot = (spots_col[:, 2, :, None] == lax.iota(jnp.int32, layers)).astype(f32)
        c_got = c_got[:, :, : slots * depth].reshape(nc, qa, slots, depth)
        drive_c = jnp.einsum("sqmk,smb->qbk", c_got, onehot, precision=HIGH).reshape(qa, length)
        pieces = [d.reshape(nr, qb, tile) for d in drive_b]
        pieces.append(fold(gram_a.reshape(nr, qb, rank)))
        send_c = jnp.swapaxes(pad_lanes(drive_c.reshape(qa, nr, ka)), 0, 1)
        pieces.append(fold(send_c))
        got = swap(jnp.concatenate(pieces, axis=1), "row")
        b_got, s_got, c_got = take(got, [qb * tiles_b, qb * half, fold(send_c).shape[1]])
        mine_b = jnp.sum(b_got, axis=0).reshape(tiles_b, qb, tile)
        sa_r = unfold(jnp.sum(s_got, axis=0), rank)
        mine_c = unfold(jnp.sum(c_got, axis=0), send_c.shape[-1])[:, :ka]
        sc_c = lax.dynamic_slice_in_dim(gram_c, col * qa, qa, 0)
        sc_r = lax.dynamic_slice_in_dim(gram_c, row * qb, qb, 0)
        old_a = lax.dynamic_slice_in_dim(at3, col * qa, qa, 1)
        old_b = lax.dynamic_slice_in_dim(bt3, row * qb, qb, 1)
        old_c = lax.dynamic_slice_in_dim(crow_t, col * qa, qa, 0)
        new_a = bump(old_a, sb_c * sc_c, at3, drive_a, step_sizes[sweep, 0])
        new_b = bump(old_b, sa_r * sc_r, bt3, mine_b, step_sizes[sweep, 1])
        new_c = bump(old_c[None], sa_c * sb_c, crow_t[None], mine_c[None], step_sizes[sweep, 2])[0]
    per_a = tile // own_a
    cut = new_a.reshape(tiles_a, qa, per_a, own_a).transpose(0, 2, 1, 3).reshape(nc, qa, own_a)
    cut = pad_lanes(jnp.concatenate([cut, jnp.broadcast_to(new_c[None], (nc, qa, ka))], axis=2))
    got = unfold(swap(fold(cut), "col"), cut.shape[-1])
    out_a = got[:, :, :own_a].reshape(rank, own_a).T
    rows_c = got[:, :, own_a : own_a + ka].reshape(rank, ka).T
    per_b = tile // own_b
    cut = new_b.reshape(tiles_b, qb, per_b, own_b).transpose(0, 2, 1, 3).reshape(nr, qb, own_b)
    cut = fold(pad_lanes(cut))
    everyone = jnp.broadcast_to(fold(rows_c)[None], (nr, ka * half, LANES))
    got = swap(jnp.concatenate([cut, everyone], axis=1), "row")
    b_got, c_got = take(got, [cut.shape[1], ka * half])
    out_b = unfold(b_got, own_b + -own_b % LANES)[:, :, :own_b].reshape(rank, own_b).T
    out_c = unfold(c_got, rank).reshape(length, rank)
    return out_a[None], out_b[None], out_c


def solution(mesh):
    placed = (
        P("row", "col", None, None, None, None),
        P("row", "col", None, None),
        P("row", "col"),
        P(),
        P("row", "col", None),
        P("col", "row", None),
        P(),
    )
    return jax.shard_map(
        shards,
        mesh=mesh,
        in_specs=placed,
        out_specs=(P("row", "col", None), P("col", "row", None), P()),
        check_vma=False,
    )
```

```python
import jax
import jax.numpy as jnp
from jax import lax
from jax.sharding import PartitionSpec as P

LANES = 128
HIGH = lax.Precision.HIGHEST


def swap(x, axis):
    return lax.all_to_all(x, axis, 0, 0, tiled=True)


def spread(x, peers):
    return lax.optimization_barrier(jnp.broadcast_to(x[None], (peers,) + x.shape))


def pad_lanes(x):
    short = -x.shape[-1] % LANES
    return jnp.pad(x, [(0, 0)] * (x.ndim - 1) + [(0, short)])


def fold(x):
    lead, (m, n) = x.shape[:-2], x.shape[-2:]
    parts = [x[..., t * LANES : (t + 1) * LANES] for t in range(n // LANES)]
    return jnp.concatenate(parts, axis=-2)


def unfold(x, n):
    tiles = n // LANES
    m = x.shape[-2] // tiles
    return jnp.concatenate([x[..., t * m : (t + 1) * m, :] for t in range(tiles)], axis=-1)


def take(x, sizes):
    out, at = [], 0
    for size in sizes:
        out.append(x[:, at : at + size])
        at += size
    return out


def gram(values):
    return lax.dot_general(
        values, values, (((0,), (0,)), ((), ())), preferred_element_type=jnp.float32
    )


def brick_terms(brick, a_tile, b_tile, c_rows):
    c_wide = c_rows.astype(jnp.float32)[:, None, :]
    wide = jnp.einsum("kij,jq->kiq", brick, b_tile, preferred_element_type=jnp.float32)
    along_a = jnp.sum(wide * c_wide, axis=0)
    deep = jnp.einsum("kij,iq->kjq", brick, a_tile, preferred_element_type=jnp.float32)
    along_b = jnp.sum(deep * c_wide, axis=0)
    along_c = jnp.sum(deep * b_tile.astype(jnp.float32)[None, :, :], axis=1)
    return along_a, along_b, along_c


def bump(state, hess, full, drive, rate):
    scale = jnp.sum(jnp.abs(hess), axis=1) + 1e-06
    push = jnp.stack(
        [jnp.dot(hess, f, precision=HIGH, preferred_element_type=jnp.float32) for f in full]
    )
    return jnp.maximum(state - rate * (push - drive) / scale[None, :, None], 0.0)


def bump_rows(state, hess, drive, rate):
    scale = jnp.sum(jnp.abs(hess), axis=1) + 1e-06
    push = jnp.dot(state, hess, precision=HIGH, preferred_element_type=jnp.float32)
    return jnp.maximum(state - rate * (push - drive) / scale[None, :], 0.0)


def lanes(x):
    return jnp.stack([x[:, t * LANES : (t + 1) * LANES] for t in range(x.shape[1] // LANES)])


def shards(bricks, brick_coords, brick_counts, step_sizes, init_a, init_b, init_c):
    nr, nc = lax.axis_size("row"), lax.axis_size("col")
    col = lax.axis_index("col")
    slab, places, own = bricks[0, 0], brick_coords[0, 0], brick_counts[0, 0]
    slots, depth, tile, _ = slab.shape
    sweeps = step_sizes.shape[0]
    rank = init_a.shape[-1]
    own_a, own_b = init_a.shape[1], init_b.shape[1]
    tiles_a, tiles_b = own_a * nc // tile, own_b * nr // tile
    length = init_c.shape[0]
    layers, tiles_c = length // depth, length // LANES
    qa, qb = rank // nc, rank // nr
    f32, bf16 = jnp.float32, jnp.bfloat16
    half = rank // LANES

    live = lax.iota(jnp.int32, slots) < own
    spots = jnp.where(live[None, :], places, 0)
    mine = pad_lanes(jnp.where(live[None, :], places, -1).astype(f32).reshape(1, -1))
    mine = jnp.broadcast_to(mine, (8, LANES))

    state_b = init_b[0]
    c_bf = init_c.astype(bf16)

    for sweep in range(sweeps):
        b_bf = state_b.astype(bf16)
        if sweep == 0:
            got = swap(spread(jnp.concatenate([fold(init_a[0]), mine], 0), nc), "col")
            rows, spots_col = take(got, [own_a * half, 8])
            a_rows = unfold(rows, rank).reshape(tiles_a, tile, rank)
            at3 = jnp.swapaxes(a_rows, 1, 2)
            a_bf3 = a_rows.astype(bf16)
            spots_col = spots_col[:, 0, : 3 * slots].reshape(nc, 3, slots).astype(jnp.int32)
            ct3 = lanes(init_c.T)
        else:
            send = jnp.concatenate([new_a.reshape(-1, LANES), new_c.reshape(-1, LANES)], 0)
            got = swap(spread(send, nc), "col")
            chunk, c_got = take(got, [tiles_a * qa, tiles_c * qa])
            at3 = jnp.swapaxes(chunk.reshape(nc, tiles_a, qa, tile), 0, 1).reshape(tiles_a, rank, tile)
            a_bf3 = jnp.swapaxes(at3.astype(bf16), 1, 2)
            ct3 = jnp.swapaxes(c_got.reshape(nc, tiles_c, qa, LANES), 0, 1).reshape(tiles_c, rank, LANES)
            c_bf = jnp.swapaxes(ct3.astype(bf16), 1, 2).reshape(length, rank)
        a_all = a_bf3.reshape(tiles_a * tile, rank)
        gram_a = gram(a_all)
        slice_a = lax.dynamic_slice_in_dim(gram_a, col * qa, qa, 0)
        slice_a = jnp.swapaxes(slice_a.reshape(qa, nr, qb), 0, 1)
        high = lax.reduce_precision(slice_a, 8, 7)
        pair = pad_lanes(jnp.concatenate([high, slice_a - high], axis=2).astype(bf16))
        send = jnp.concatenate(
            [jnp.broadcast_to(fold(b_bf)[None], (nr, own_b * half, LANES)), fold(pair)], axis=1
        )
        got = swap(send, "row")
        b_got, s_got = take(got, [own_b * half, fold(pair).shape[1]])
        b_all = unfold(b_got, rank).reshape(tiles_b * tile, rank)
        gram_b = gram(b_all)
        s_got = unfold(s_got, pair.shape[2]).astype(f32)
        piece = jnp.sum(s_got[:, :, :qb] + s_got[:, :, qb : 2 * qb], axis=0)
        gram_c = gram(c_bf)
        parts_a, parts_c = [], []
        drive_b = jnp.zeros((tiles_b, tile, rank), f32)
        for slot in range(slots):
            ti, tj, tk = spots[0, slot], spots[1, slot], spots[2, slot]
            a_tile = lax.dynamic_index_in_dim(a_bf3, ti, 0, keepdims=False)
            b_tile = lax.dynamic_slice_in_dim(b_all, tj * tile, tile, 0)
            c_rows = lax.dynamic_slice_in_dim(c_bf, tk * depth, depth, 0)
            da, db, dc = brick_terms(slab[slot], a_tile, b_tile, c_rows)
            parts_a.append(da.T)
            parts_c.append(dc.T)
            here = (lax.iota(jnp.int32, tiles_b) == tj) & live[slot]
            drive_b = drive_b + jnp.where(here[:, None, None], db[None], 0.0)
        pieces = [p.reshape(nc, qa, tile) for p in parts_a]
        pieces.append(fold(gram_b.reshape(nc, qa, rank)))
        mixed = jnp.concatenate(parts_c, axis=1).reshape(nc, qa, slots * depth)
        mixed = jnp.concatenate([mixed, jnp.broadcast_to(piece[None], (nc, qa, qb))], axis=2)
        pieces.append(fold(pad_lanes(mixed)))
        got = swap(jnp.concatenate(pieces, axis=1), "col")
        *a_got, s_got, m_got = take(got, [qa] * slots + [qa * half, pieces[-1].shape[1]])
        sb_c = unfold(jnp.sum(s_got, axis=0), rank)
        m_got = unfold(m_got, pad_lanes(mixed).shape[2])
        drive_a = jnp.stack(
            [
                sum(
                    jnp.sum(jnp.where((spots_col[:, 0, m] == t)[:, None, None], a_got[m], 0.0), axis=0)
                    for m in range(slots)
                )
                for t in range(tiles_a)
            ]
        )
        onehot = (spots_col[:, 2, :, None] == lax.iota(jnp.int32, layers)).astype(f32)
        c_got = m_got[:, :, : slots * depth].reshape(nc, qa, slots, depth)
        drive_c = jnp.einsum("sqmk,smb->qbk", c_got, onehot, precision=HIGH).reshape(qa, length)
        strip = m_got[:, :, slots * depth : slots * depth + qb].reshape(rank, qb).T
        pieces = [
            fold(drive_b.reshape(nr, own_b, rank)),
            jnp.broadcast_to(fold(strip)[None], (nr, qb * half, LANES)),
            jnp.broadcast_to(fold(drive_c)[None], (nr, qa * tiles_c, LANES)),
        ]
        got = swap(jnp.concatenate(pieces, axis=1), "row")
        b_got, s_got, c_got = take(got, [p.shape[1] for p in pieces])
        mine_b = unfold(jnp.sum(b_got, axis=0), rank)
        sa = unfold(s_got, rank).reshape(rank, rank)
        mine_c = jnp.sum(c_got, axis=0).reshape(tiles_c, qa, LANES)
        cut = lambda x, axis=0: lax.dynamic_slice_in_dim(x, col * qa, qa, axis)
        rate = step_sizes[sweep]
        new_a = bump(cut(at3, 1), sb_c * cut(gram_c), at3, drive_a, rate[0])
        state_b = bump_rows(state_b, sa * gram_c, mine_b, rate[1])
        new_c = bump(cut(ct3, 1), cut(sa) * sb_c, ct3, mine_c, rate[2])
    per_a = tile // own_a
    own = new_a.reshape(tiles_a, qa, per_a, own_a).transpose(0, 2, 1, 3).reshape(nc, qa, own_a)
    own = fold(pad_lanes(own))
    everyone = jnp.broadcast_to(new_c.reshape(1, -1, LANES), (nc, qa * tiles_c, LANES))
    got = swap(jnp.concatenate([own, everyone], axis=1), "col")
    a_got, c_got = take(got, [own.shape[1], qa * tiles_c])
    out_a = unfold(a_got, own_a + -own_a % LANES)[:, :, :own_a].reshape(rank, own_a).T
    out_c = jnp.swapaxes(c_got.reshape(nc, tiles_c, qa, LANES), 0, 1).reshape(tiles_c, rank, LANES)
    out_c = jnp.swapaxes(out_c, 1, 2).reshape(length, rank)
    return out_a[None], state_b[None], out_c


def solution(mesh):
    placed = (
        P("row", "col", None, None, None, None),
        P("row", "col", None, None),
        P("row", "col"),
        P(),
        P("row", "col", None),
        P("col", "row", None),
        P(),
    )
    return jax.shard_map(
        shards,
        mesh=mesh,
        in_specs=placed,
        out_specs=(P("row", "col", None), P("col", "row", None), P()),
        check_vma=False,
    )
```

```python
import jax
import jax.numpy as jnp
from jax import lax
from jax.experimental import pallas as pl
from jax.experimental.pallas import tpu as pltpu
from jax.sharding import PartitionSpec as P

LANES = 128
HIGH = lax.Precision.HIGHEST


def swap(x, axis):
    return lax.all_to_all(x, axis, 0, 0, tiled=True)


def spread(x, peers):
    return lax.optimization_barrier(jnp.broadcast_to(x[None], (peers,) + x.shape))


def pad_lanes(x):
    short = -x.shape[-1] % LANES
    return jnp.pad(x, [(0, 0)] * (x.ndim - 1) + [(0, short)])


def fold(x):
    lead, (m, n) = x.shape[:-2], x.shape[-2:]
    parts = [x[..., t * LANES : (t + 1) * LANES] for t in range(n // LANES)]
    return jnp.concatenate(parts, axis=-2)


def unfold(x, n):
    tiles = n // LANES
    m = x.shape[-2] // tiles
    return jnp.concatenate([x[..., t * m : (t + 1) * m, :] for t in range(tiles)], axis=-1)


def take(x, sizes):
    out, at = [], 0
    for size in sizes:
        out.append(x[:, at : at + size])
        at += size
    return out


def gram(values):
    return lax.dot_general(
        values, values, (((0,), (0,)), ((), ())), preferred_element_type=jnp.float32
    )


def deep_kernel(meta, slab, a_ref, c_ref, out, drive):
    slots, depth, tile, _ = slab.shape
    nr, rows, _ = out.shape
    half = a_ref.shape[2] // LANES
    own = rows // half
    drive[...] = jnp.zeros_like(drive)
    for slot in range(slots):
        a_tile = a_ref[meta[0, slot]]
        c_rows = c_ref[pl.ds(pl.multiple_of(meta[2, slot] * depth, depth), depth), :]
        c_rows = c_rows.astype(jnp.float32)
        total = jnp.zeros(a_tile.shape, jnp.float32)
        for k in range(depth):
            deep = lax.dot_general(
                slab[slot, k], a_tile, (((0,), (0,)), ((), ())),
                preferred_element_type=jnp.float32,
            )
            total = total + deep * c_rows[k : k + 1, :]
        spot = pl.ds(pl.multiple_of(meta[1, slot] * tile, tile), tile)
        drive[spot, :] = drive[spot, :] + jnp.where(meta[3, slot] > 0, total, 0.0)
    for h in range(half):
        part = drive[:, h * LANES : (h + 1) * LANES]
        out[:, own * h : own * (h + 1), :] = part.reshape(nr, own, LANES)


def wide_kernel(meta, got, slab, a_ref, c_ref, out, b_all, deep_c):
    slots, depth, tile, _ = slab.shape
    nr = got.shape[0]
    nc = out.shape[0]
    rank = a_ref.shape[2]
    half, qa, qb = rank // LANES, rank // nc, rank // nr
    own = b_all.shape[0] // nr
    for h in range(half):
        part = got[:, own * h : own * (h + 1), :]
        b_all[:, h * LANES : (h + 1) * LANES] = part.reshape(nr * own, LANES)
    deep_c[...] = jnp.zeros_like(deep_c)
    for slot in range(slots):
        b_tile = b_all[pl.ds(pl.multiple_of(meta[1, slot] * tile, tile), tile), :]
        a_tile = a_ref[meta[0, slot]].astype(jnp.float32)
        c_rows = c_ref[pl.ds(pl.multiple_of(meta[2, slot] * depth, depth), depth), :]
        c_rows = c_rows.astype(jnp.float32)
        total = jnp.zeros((tile, rank), jnp.float32)
        for k in range(depth):
            wide = jnp.dot(slab[slot, k], b_tile, preferred_element_type=jnp.float32)
            total = total + wide * c_rows[k : k + 1, :]
            deep_c[slot * depth + k : slot * depth + k + 1, :] = jnp.sum(
                wide * a_tile, axis=0, keepdims=True
            )
        out[:, slot * qa : (slot + 1) * qa, :] = total.T.reshape(nc, qa, LANES)
    at = slots * qa
    whole = b_all[...]
    gram_b = lax.dot_general(
        whole, whole, (((0,), (0,)), ((), ())), preferred_element_type=jnp.float32
    )
    for h in range(half):
        part = gram_b[:, h * LANES : (h + 1) * LANES]
        out[:, at : at + qa, :] = part.reshape(nc, qa, LANES)
        at += qa
    pieces = got[:, own * half : own * half + qa, :].astype(jnp.float32)
    piece = jnp.sum(pieces, axis=0)
    first = slots * depth
    moved = pltpu.roll(piece, first, 1) + pltpu.roll(piece, first - qb, 1)
    lane = lax.broadcasted_iota(jnp.int32, piece.shape, 1)
    moved = jnp.where((lane >= first) & (lane < first + qb), moved, 0.0)
    out[:, at : at + qa, :] = deep_c[...].T.reshape(nc, qa, LANES) + moved[None]


def call(kernel, shape, scratch, flops, moved, operands):
    memory = [pltpu.SMEM] + [pltpu.VMEM] * (len(operands) - 1)
    return pl.pallas_call(
        kernel,
        out_shape=jax.ShapeDtypeStruct(shape, jnp.float32),
        in_specs=[pl.BlockSpec(memory_space=m) for m in memory],
        out_specs=pl.BlockSpec(memory_space=pltpu.VMEM),
        scratch_shapes=scratch,
        cost_estimate=pl.CostEstimate(flops=flops, bytes_accessed=moved, transcendentals=0),
        compiler_params=pltpu.CompilerParams(vmem_limit_bytes=32 << 20),
    )(*operands)


def bump(state, hess, full, drive, rate):
    scale = jnp.sum(jnp.abs(hess), axis=1) + 1e-06
    push = jnp.stack(
        [jnp.dot(hess, f, precision=HIGH, preferred_element_type=jnp.float32) for f in full]
    )
    return jnp.maximum(state - rate * (push - drive) / scale[None, :, None], 0.0)


def bump_rows(state, hess, drive, rate):
    scale = jnp.sum(jnp.abs(hess), axis=1) + 1e-06
    push = jnp.dot(state, hess, precision=HIGH, preferred_element_type=jnp.float32)
    return jnp.maximum(state - rate * (push - drive) / scale[None, :], 0.0)


def lanes(x):
    return jnp.stack([x[:, t * LANES : (t + 1) * LANES] for t in range(x.shape[1] // LANES)])


def shards(bricks, brick_coords, brick_counts, step_sizes, init_a, init_b, init_c):
    nr, nc = lax.axis_size("row"), lax.axis_size("col")
    col = lax.axis_index("col")
    slab, places, own = bricks[0, 0], brick_coords[0, 0], brick_counts[0, 0]
    slots, depth, tile, _ = slab.shape
    sweeps = step_sizes.shape[0]
    rank = init_a.shape[-1]
    own_a, own_b = init_a.shape[1], init_b.shape[1]
    tiles_a, tiles_b = own_a * nc // tile, own_b * nr // tile
    length = init_c.shape[0]
    layers, tiles_c = length // depth, length // LANES
    qa, qb = rank // nc, rank // nr
    f32, bf16 = jnp.float32, jnp.bfloat16
    half = rank // LANES

    live = lax.iota(jnp.int32, slots) < own
    meta = jnp.concatenate(
        [jnp.where(live[None, :], places, 0), live[None, :].astype(jnp.int32)], axis=0
    )
    mine = pad_lanes(jnp.where(live[None, :], places, -1).astype(f32).reshape(1, -1))
    mine = jnp.broadcast_to(mine, (8, LANES))

    state_b = init_b[0]
    c_bf = init_c.astype(bf16)

    for sweep in range(sweeps):
        b_bf = state_b.astype(bf16)
        if sweep == 0:
            got = swap(spread(jnp.concatenate([fold(init_a[0]), mine], 0), nc), "col")
            rows, spots_col = take(got, [own_a * half, 8])
            a_rows = unfold(rows, rank).reshape(tiles_a, tile, rank)
            at3 = jnp.swapaxes(a_rows, 1, 2)
            a_bf3 = a_rows.astype(bf16)
            spots_col = spots_col[:, 0, : 3 * slots].reshape(nc, 3, slots).astype(jnp.int32)
            ct3 = lanes(init_c.T)
        else:
            send = jnp.concatenate([new_a.reshape(-1, LANES), new_c.reshape(-1, LANES)], 0)
            got = swap(spread(send, nc), "col")
            chunk, c_got = take(got, [tiles_a * qa, tiles_c * qa])
            at3 = jnp.swapaxes(chunk.reshape(nc, tiles_a, qa, tile), 0, 1).reshape(tiles_a, rank, tile)
            a_bf3 = jnp.swapaxes(at3.astype(bf16), 1, 2)
            ct3 = jnp.swapaxes(c_got.reshape(nc, tiles_c, qa, LANES), 0, 1).reshape(tiles_c, rank, LANES)
            c_bf = jnp.swapaxes(ct3.astype(bf16), 1, 2).reshape(length, rank)
        a_all = a_bf3.reshape(tiles_a * tile, rank)
        gram_a = gram(a_all)
        slice_a = lax.dynamic_slice_in_dim(gram_a, col * qa, qa, 0)
        slice_a = jnp.swapaxes(slice_a.reshape(qa, nr, qb), 0, 1)
        high = lax.reduce_precision(slice_a, 8, 7)
        pair = pad_lanes(jnp.concatenate([high, slice_a - high], axis=2).astype(bf16))
        send = jnp.concatenate(
            [jnp.broadcast_to(fold(b_bf)[None], (nr, own_b * half, LANES)), fold(pair)], axis=1
        )
        got = swap(send, "row")
        gram_c = gram(c_bf)
        work = 2 * slots * depth * tile * tile * rank
        blocks = call(
            deep_kernel,
            (nr, own_b * half, LANES),
            [pltpu.VMEM((tiles_b * tile, rank), f32)],
            work, slab.size * 2, (meta, slab, a_bf3, c_bf),
        )
        send = call(
            wide_kernel,
            (nc, qa * (slots + half + 1), LANES),
            [pltpu.VMEM((tiles_b * tile, rank), bf16), pltpu.VMEM((LANES, rank), f32)],
            work, slab.size * 2, (meta, got, slab, a_bf3, c_bf),
        )
        got = swap(send, "col")
        *a_got, s_got, m_got = take(got, [qa] * slots + [qa * half, qa])
        sb_c = unfold(jnp.sum(s_got, axis=0), rank)
        drive_a = jnp.stack(
            [
                sum(
                    jnp.sum(jnp.where((spots_col[:, 0, m] == t)[:, None, None], a_got[m], 0.0), axis=0)
                    for m in range(slots)
                )
                for t in range(tiles_a)
            ]
        )
        onehot = (spots_col[:, 2, :, None] == lax.iota(jnp.int32, layers)).astype(f32)
        c_got = m_got[:, :, : slots * depth].reshape(nc, qa, slots, depth)
        drive_c = jnp.einsum("sqmk,smb->qbk", c_got, onehot, precision=HIGH).reshape(qa, length)
        strip = m_got[:, :, slots * depth : slots * depth + qb].reshape(rank, qb).T
        pieces = [
            blocks,
            jnp.broadcast_to(fold(strip)[None], (nr, qb * half, LANES)),
            jnp.broadcast_to(fold(drive_c)[None], (nr, qa * tiles_c, LANES)),
        ]
        got = swap(jnp.concatenate(pieces, axis=1), "row")
        b_got, s_got, c_got = take(got, [p.shape[1] for p in pieces])
        mine_b = unfold(jnp.sum(b_got, axis=0), rank)
        sa = unfold(s_got, rank).reshape(rank, rank)
        mine_c = jnp.sum(c_got, axis=0).reshape(tiles_c, qa, LANES)
        cut = lambda x, axis=0: lax.dynamic_slice_in_dim(x, col * qa, qa, axis)
        rate = step_sizes[sweep]
        new_a = bump(cut(at3, 1), sb_c * cut(gram_c), at3, drive_a, rate[0])
        state_b = bump_rows(state_b, sa * gram_c, mine_b, rate[1])
        new_c = bump(cut(ct3, 1), cut(sa) * sb_c, ct3, mine_c, rate[2])
    per_a = tile // own_a
    own = new_a.reshape(tiles_a, qa, per_a, own_a).transpose(0, 2, 1, 3).reshape(nc, qa, own_a)
    own = fold(pad_lanes(own))
    everyone = jnp.broadcast_to(new_c.reshape(1, -1, LANES), (nc, qa * tiles_c, LANES))
    got = swap(jnp.concatenate([own, everyone], axis=1), "col")
    a_got, c_got = take(got, [own.shape[1], qa * tiles_c])
    out_a = unfold(a_got, own_a + -own_a % LANES)[:, :, :own_a].reshape(rank, own_a).T
    out_c = jnp.swapaxes(c_got.reshape(nc, tiles_c, qa, LANES), 0, 1).reshape(tiles_c, rank, LANES)
    out_c = jnp.swapaxes(out_c, 1, 2).reshape(length, rank)
    return out_a[None], state_b[None], out_c


def solution(mesh):
    placed = (
        P("row", "col", None, None, None, None),
        P("row", "col", None, None),
        P("row", "col"),
        P(),
        P("row", "col", None),
        P("col", "row", None),
        P(),
    )
    return jax.shard_map(
        shards,
        mesh=mesh,
        in_specs=placed,
        out_specs=(P("row", "col", None), P("col", "row", None), P()),
        check_vma=False,
    )
```

```python
import jax
import jax.numpy as jnp
from jax import lax
from jax.experimental import pallas as pl
from jax.experimental.pallas import tpu as pltpu
from jax.sharding import PartitionSpec as P

LANES = 128
HIGH = lax.Precision.HIGHEST


def swap(x, axis):
    return lax.all_to_all(x, axis, 0, 0, tiled=True)


def spread(x, peers):
    return lax.optimization_barrier(jnp.broadcast_to(x[None], (peers,) + x.shape))


def pad_lanes(x):
    short = -x.shape[-1] % LANES
    return jnp.pad(x, [(0, 0)] * (x.ndim - 1) + [(0, short)])


def fold(x):
    lead, (m, n) = x.shape[:-2], x.shape[-2:]
    parts = [x[..., t * LANES : (t + 1) * LANES] for t in range(n // LANES)]
    return jnp.concatenate(parts, axis=-2)


def unfold(x, n):
    tiles = n // LANES
    m = x.shape[-2] // tiles
    return jnp.concatenate([x[..., t * m : (t + 1) * m, :] for t in range(tiles)], axis=-1)


def take(x, sizes):
    out, at = [], 0
    for size in sizes:
        out.append(x[:, at : at + size])
        at += size
    return out


def gram(values):
    return lax.dot_general(
        values, values, (((0,), (0,)), ((), ())), preferred_element_type=jnp.float32
    )


def deep_kernel(meta, slab, a_ref, c_ref, out, drive):
    slots, depth, tile, _ = slab.shape
    nr, rows, _ = out.shape
    tiles = drive.shape[0] // tile
    own = rows // tiles
    drive[...] = jnp.zeros_like(drive)
    for slot in range(slots):
        a_tile = a_ref[meta[0, slot]]
        c_rows = c_ref[pl.ds(pl.multiple_of(meta[2, slot] * depth, depth), depth), :]
        c_rows = c_rows.astype(jnp.float32)
        total = jnp.zeros(a_tile.shape, jnp.float32)
        for k in range(depth):
            deep = lax.dot_general(
                slab[slot, k], a_tile, (((0,), (0,)), ((), ())),
                preferred_element_type=jnp.float32,
            )
            total = total + deep * c_rows[k : k + 1, :]
        spot = pl.ds(pl.multiple_of(meta[1, slot] * tile, tile), tile)
        drive[spot, :] = drive[spot, :] + jnp.where(meta[3, slot] > 0, total, 0.0)
    for t in range(tiles):
        part = drive[t * tile : (t + 1) * tile, :].T
        out[:, own * t : own * (t + 1), :] = part.reshape(nr, own, LANES)


def wide_kernel(meta, b_all, slab, a_ref, c_ref, out, deep_c):
    slots, depth, tile, _ = slab.shape
    nc = out.shape[0]
    rank = a_ref.shape[2]
    half, qa = rank // LANES, rank // nc
    deep_c[...] = jnp.zeros_like(deep_c)
    for slot in range(slots):
        b_tile = b_all[pl.ds(pl.multiple_of(meta[1, slot] * tile, tile), tile), :]
        a_tile = a_ref[meta[0, slot]].astype(jnp.float32)
        c_rows = c_ref[pl.ds(pl.multiple_of(meta[2, slot] * depth, depth), depth), :]
        c_rows = c_rows.astype(jnp.float32)
        total = jnp.zeros((tile, rank), jnp.float32)
        for k in range(depth):
            wide = jnp.dot(slab[slot, k], b_tile, preferred_element_type=jnp.float32)
            total = total + wide * c_rows[k : k + 1, :]
            deep_c[slot * depth + k : slot * depth + k + 1, :] = jnp.sum(
                wide * a_tile, axis=0, keepdims=True
            )
        out[:, slot * qa : (slot + 1) * qa, :] = total.T.reshape(nc, qa, LANES)
    at = slots * qa
    whole = b_all[...]
    gram_b = lax.dot_general(
        whole, whole, (((0,), (0,)), ((), ())), preferred_element_type=jnp.float32
    )
    for h in range(half):
        part = gram_b[:, h * LANES : (h + 1) * LANES]
        out[:, at : at + qa, :] = part.reshape(nc, qa, LANES)
        at += qa
    out[:, at : at + qa, :] = deep_c[...].T.reshape(nc, qa, LANES)


def call(kernel, shape, scratch, flops, moved, operands):
    memory = [pltpu.SMEM] + [pltpu.VMEM] * (len(operands) - 1)
    return pl.pallas_call(
        kernel,
        out_shape=jax.ShapeDtypeStruct(shape, jnp.float32),
        in_specs=[pl.BlockSpec(memory_space=m) for m in memory],
        out_specs=pl.BlockSpec(memory_space=pltpu.VMEM),
        scratch_shapes=scratch,
        cost_estimate=pl.CostEstimate(flops=flops, bytes_accessed=moved, transcendentals=0),
        compiler_params=pltpu.CompilerParams(vmem_limit_bytes=32 << 20),
    )(*operands)


def bump(state, hess, full, drive, rate):
    scale = jnp.sum(jnp.abs(hess), axis=1) + 1e-06
    push = jnp.stack(
        [jnp.dot(hess, f, precision=HIGH, preferred_element_type=jnp.float32) for f in full]
    )
    return jnp.maximum(state - rate * (push - drive) / scale[None, :, None], 0.0)


def steps_of(n):
    masks = [1 << b for b in range(n.bit_length() - 1)]
    return masks[::-1][::2] + masks[::-1][1::2]


def flip(x, axis, mask):
    n = lax.axis_size(axis)
    return lax.ppermute(x, axis, [(i, i ^ mask) for i in range(n)])


def ordered(x, order, n):
    masks = order[::-1]
    dims = [masks.index(m) for m in sorted(masks, reverse=True)]
    rest = list(range(len(masks), x.ndim))
    return x.transpose(dims + rest).reshape((n,) + x.shape[len(masks) :])


def gather_by_flips(x, axis):
    n, me = lax.axis_size(axis), lax.axis_index(axis)
    order = steps_of(n)
    for mask in order:
        y = flip(x, axis, mask)
        upper = (me & mask) > 0
        x = jnp.stack([jnp.where(upper, y, x), jnp.where(upper, x, y)])
    return ordered(x, order, n)


def swap_by_flips(x, axis):
    n, me = lax.axis_size(axis), lax.axis_index(axis)
    order = steps_of(n)
    bits = n.bit_length() - 1
    masks = sorted(order, reverse=True)
    rest = x.shape[1:]
    x = x.reshape((2,) * bits + rest)
    left = list(masks)
    for mask in order:
        at = len(masks) - len(left) + left.index(mask)
        upper = (me & mask) > 0
        zero, one = lax.index_in_dim(x, 0, at, False), lax.index_in_dim(x, 1, at, False)
        y = flip(jnp.where(upper, zero, one), axis, mask)
        keep = jnp.where(upper, one, zero)
        x = jnp.stack([jnp.where(upper, y, keep), jnp.where(upper, keep, y)])
        left.remove(mask)
    return ordered(x, order, n)


def lanes(x):
    return jnp.stack([x[:, t * LANES : (t + 1) * LANES] for t in range(x.shape[1] // LANES)])


def shards(bricks, brick_coords, brick_counts, step_sizes, init_a, init_b, init_c):
    nr, nc = lax.axis_size("row"), lax.axis_size("col")
    row, col = lax.axis_index("row"), lax.axis_index("col")
    slab, places, own = bricks[0, 0], brick_coords[0, 0], brick_counts[0, 0]
    slots, depth, tile, _ = slab.shape
    sweeps = step_sizes.shape[0]
    rank = init_a.shape[-1]
    own_a, own_b = init_a.shape[1], init_b.shape[1]
    tiles_a, tiles_b = own_a * nc // tile, own_b * nr // tile
    length = init_c.shape[0]
    layers, tiles_c = length // depth, length // LANES
    qa, qb = rank // nc, rank // nr
    f32, bf16 = jnp.float32, jnp.bfloat16
    half = rank // LANES

    live = lax.iota(jnp.int32, slots) < own
    meta = jnp.concatenate(
        [jnp.where(live[None, :], places, 0), live[None, :].astype(jnp.int32)], axis=0
    )
    mine = pad_lanes(jnp.where(live[None, :], places, -1).astype(f32).reshape(1, -1))
    mine = jnp.broadcast_to(mine, (8, LANES))

    c_bf = init_c.astype(bf16)

    for sweep in range(sweeps):
        if sweep == 0:
            b_rows = gather_by_flips(init_b[0], "row").reshape(tiles_b, tile, rank)
            bt3 = jnp.swapaxes(b_rows, 1, 2)
        else:
            chunk = gather_by_flips(new_b.reshape(-1, LANES), "row")
            bt3 = jnp.swapaxes(chunk.reshape(nr, tiles_b, qb, tile), 0, 1).reshape(tiles_b, rank, tile)
            b_rows = jnp.swapaxes(bt3, 1, 2)
        b_all = b_rows.reshape(tiles_b * tile, rank).astype(bf16)
        if sweep == 0:
            got = swap(spread(jnp.concatenate([fold(init_a[0]), mine], 0), nc), "col")
            rows, spots_col = take(got, [own_a * half, 8])
            a_rows = unfold(rows, rank).reshape(tiles_a, tile, rank)
            at3 = jnp.swapaxes(a_rows, 1, 2)
            a_bf3 = a_rows.astype(bf16)
            spots_col = spots_col[:, 0, : 3 * slots].reshape(nc, 3, slots).astype(jnp.int32)
            ct3 = lanes(init_c.T)
        else:
            send = jnp.concatenate([new_a.reshape(-1, LANES), new_c.reshape(-1, LANES)], 0)
            got = swap(spread(send, nc), "col")
            chunk, c_got = take(got, [tiles_a * qa, tiles_c * qa])
            at3 = jnp.swapaxes(chunk.reshape(nc, tiles_a, qa, tile), 0, 1).reshape(tiles_a, rank, tile)
            a_bf3 = jnp.swapaxes(at3.astype(bf16), 1, 2)
            ct3 = jnp.swapaxes(c_got.reshape(nc, tiles_c, qa, LANES), 0, 1).reshape(tiles_c, rank, LANES)
            c_bf = jnp.swapaxes(ct3.astype(bf16), 1, 2).reshape(length, rank)
        a_all = a_bf3.reshape(tiles_a * tile, rank)
        gram_a = gram(a_all)
        slice_a = lax.dynamic_slice_in_dim(gram_a, col * qa, qa, 0)
        gram_c = gram(c_bf)
        work = 2 * slots * depth * tile * tile * rank
        blocks = call(
            deep_kernel,
            (nr, tiles_b * qb, LANES),
            [pltpu.VMEM((tiles_b * tile, rank), f32)],
            work, slab.size * 2, (meta, slab, a_bf3, c_bf),
        )
        send = call(
            wide_kernel,
            (nc, qa * (slots + half + 1), LANES),
            [pltpu.VMEM((LANES, rank), f32)],
            work, slab.size * 2, (meta, b_all, slab, a_bf3, c_bf),
        )
        got = swap(send, "col")
        *a_got, s_got, m_got = take(got, [qa] * slots + [qa * half, qa])
        sb_c = unfold(jnp.sum(s_got, axis=0), rank)
        drive_a = jnp.stack(
            [
                sum(
                    jnp.sum(jnp.where((spots_col[:, 0, m] == t)[:, None, None], a_got[m], 0.0), axis=0)
                    for m in range(slots)
                )
                for t in range(tiles_a)
            ]
        )
        onehot = (spots_col[:, 2, :, None] == lax.iota(jnp.int32, layers)).astype(f32)
        c_got = m_got[:, :, : slots * depth].reshape(nc, qa, slots, depth)
        drive_c = jnp.einsum("sqmk,smb->qbk", c_got, onehot, precision=HIGH).reshape(qa, length)
        pieces = [
            blocks,
            fold(gram_a.reshape(nr, qb, rank)),
            jnp.broadcast_to(fold(slice_a)[None], (nr, qa * half, LANES)),
            jnp.broadcast_to(fold(drive_c)[None], (nr, qa * tiles_c, LANES)),
        ]
        got = swap(jnp.concatenate(pieces, axis=1), "row")
        total = jnp.sum(got, axis=0)[None]
        b_got, r_got, s_got, c_got = [v[0] for v in take(total, [p.shape[1] for p in pieces])]
        mine_b = b_got.reshape(tiles_b, qb, tile)
        sa_r, sa_c = unfold(r_got, rank), unfold(s_got, rank)
        mine_c = c_got.reshape(tiles_c, qa, LANES)
        cut = lambda x, axis=0: lax.dynamic_slice_in_dim(x, col * qa, qa, axis)
        cut_r = lambda x, axis=0: lax.dynamic_slice_in_dim(x, row * qb, qb, axis)
        rate = step_sizes[sweep]
        new_a = bump(cut(at3, 1), sb_c * cut(gram_c), at3, drive_a, rate[0])
        new_b = bump(cut_r(bt3, 1), sa_r * cut_r(gram_c), bt3, mine_b, rate[1])
        new_c = bump(cut(ct3, 1), sa_c * sb_c, ct3, mine_c, rate[2])
    per_b = tile // own_b
    own = new_b.reshape(tiles_b, qb, per_b, own_b).transpose(0, 2, 1, 3).reshape(nr, -1, LANES)
    out_b = swap_by_flips(own, "row").reshape(rank, own_b).T
    per_a = tile // own_a
    own = new_a.reshape(tiles_a, qa, per_a, own_a).transpose(0, 2, 1, 3).reshape(nc, qa, own_a)
    own = fold(pad_lanes(own))
    everyone = jnp.broadcast_to(new_c.reshape(1, -1, LANES), (nc, qa * tiles_c, LANES))
    got = swap(jnp.concatenate([own, everyone], axis=1), "col")
    a_got, c_got = take(got, [own.shape[1], qa * tiles_c])
    out_a = unfold(a_got, own_a + -own_a % LANES)[:, :, :own_a].reshape(rank, own_a).T
    out_c = jnp.swapaxes(c_got.reshape(nc, tiles_c, qa, LANES), 0, 1).reshape(tiles_c, rank, LANES)
    out_c = jnp.swapaxes(out_c, 1, 2).reshape(length, rank)
    return out_a[None], out_b[None], out_c


def solution(mesh):
    placed = (
        P("row", "col", None, None, None, None),
        P("row", "col", None, None),
        P("row", "col"),
        P(),
        P("row", "col", None),
        P("col", "row", None),
        P(),
    )
    return jax.shard_map(
        shards,
        mesh=mesh,
        in_specs=placed,
        out_specs=(P("row", "col", None), P("col", "row", None), P()),
        check_vma=False,
    )
```

```python
import functools

import jax
import jax.numpy as jnp
from jax import lax
from jax.experimental import pallas as pl
from jax.experimental.pallas import tpu as pltpu
from jax.sharding import PartitionSpec as P

LANES = 128
HIGH = lax.Precision.HIGHEST


def swap(x, axis):
    return lax.all_to_all(x, axis, 0, 0, tiled=True)


def spread(x, peers):
    return lax.optimization_barrier(jnp.broadcast_to(x[None], (peers,) + x.shape))


def pad_lanes(x):
    short = -x.shape[-1] % LANES
    return jnp.pad(x, [(0, 0)] * (x.ndim - 1) + [(0, short)])


def fold(x):
    lead, (m, n) = x.shape[:-2], x.shape[-2:]
    parts = [x[..., t * LANES : (t + 1) * LANES] for t in range(n // LANES)]
    return jnp.concatenate(parts, axis=-2)


def unfold(x, n):
    tiles = n // LANES
    m = x.shape[-2] // tiles
    return jnp.concatenate([x[..., t * m : (t + 1) * m, :] for t in range(tiles)], axis=-1)


def take(x, sizes):
    out, at = [], 0
    for size in sizes:
        out.append(x[:, at : at + size])
        at += size
    return out


def gram(values):
    return lax.dot_general(
        values, values, (((0,), (0,)), ((), ())), preferred_element_type=jnp.float32
    )


def deep_kernel(meta, slab, a_ref, c_ref, out, drive):
    slots, depth, tile, _ = slab.shape
    nr, rows, _ = out.shape
    half = a_ref.shape[2] // LANES
    own = rows // half
    drive[...] = jnp.zeros_like(drive)
    for slot in range(slots):
        a_tile = a_ref[meta[0, slot]]
        c_rows = c_ref[pl.ds(pl.multiple_of(meta[2, slot] * depth, depth), depth), :]
        c_rows = c_rows.astype(jnp.float32)
        total = jnp.zeros(a_tile.shape, jnp.float32)
        for k in range(depth):
            deep = lax.dot_general(
                slab[slot, k], a_tile, (((0,), (0,)), ((), ())),
                preferred_element_type=jnp.float32,
            )
            total = total + deep * c_rows[k : k + 1, :]
        spot = pl.ds(pl.multiple_of(meta[1, slot] * tile, tile), tile)
        drive[spot, :] = drive[spot, :] + jnp.where(meta[3, slot] > 0, total, 0.0)
    for h in range(half):
        part = drive[:, h * LANES : (h + 1) * LANES]
        out[:, own * h : own * (h + 1), :] = part.reshape(nr, own, LANES)


def wide_kernel(meta, got, slab, a_ref, c_ref, out, b_all, deep_c):
    slots, depth, tile, _ = slab.shape
    nr = got.shape[0]
    nc = out.shape[0]
    rank = a_ref.shape[2]
    half, qa, qb = rank // LANES, rank // nc, rank // nr
    own = b_all.shape[0] // nr
    for h in range(half):
        part = got[:, own * h : own * (h + 1), :]
        b_all[:, h * LANES : (h + 1) * LANES] = part.reshape(nr * own, LANES)
    deep_c[...] = jnp.zeros_like(deep_c)
    for slot in range(slots):
        b_tile = b_all[pl.ds(pl.multiple_of(meta[1, slot] * tile, tile), tile), :]
        a_tile = a_ref[meta[0, slot]].astype(jnp.float32)
        c_rows = c_ref[pl.ds(pl.multiple_of(meta[2, slot] * depth, depth), depth), :]
        c_rows = c_rows.astype(jnp.float32)
        total = jnp.zeros((tile, rank), jnp.float32)
        for k in range(depth):
            wide = jnp.dot(slab[slot, k], b_tile, preferred_element_type=jnp.float32)
            total = total + wide * c_rows[k : k + 1, :]
            deep_c[slot * depth + k : slot * depth + k + 1, :] = jnp.sum(
                wide * a_tile, axis=0, keepdims=True
            )
        out[:, slot * qa : (slot + 1) * qa, :] = total.T.reshape(nc, qa, LANES)
    whole = b_all[...]
    gram_b = lax.dot_general(
        whole, whole, (((0,), (0,)), ((), ())), preferred_element_type=jnp.float32
    )
    row = meta[4, 0]
    per = LANES // qb
    strip = gram_b[:, :LANES]
    for h in range(1, half):
        strip = jnp.where(row // per == h, gram_b[:, h * LANES : (h + 1) * LANES], strip)
    first = slots * depth
    second = first + qb
    third = second + qb
    strip = pltpu.roll(strip, (second + LANES - qb * (row % per)) % LANES, 1)
    pieces = got[:, own * half : own * half + qa, :].astype(jnp.float32)
    piece = jnp.sum(pieces, axis=0)
    moved = pltpu.roll(piece, first, 1) + pltpu.roll(piece, first - qb, 1)
    lane = lax.broadcasted_iota(jnp.int32, piece.shape, 1)
    spots = jnp.zeros(piece.shape, jnp.int32)
    for m in range(slots):
        alive = meta[3, m] > 0
        spots = jnp.where(lane == third + m, jnp.where(alive, meta[0, m], -1), spots)
        spots = jnp.where(lane == third + slots + m, jnp.where(alive, meta[2, m], -1), spots)
    moved = jnp.where((lane >= first) & (lane < second), moved, spots.astype(jnp.float32))
    wide_lane = lax.broadcasted_iota(jnp.int32, strip.shape, 1)
    mixed = deep_c[...].T
    mixed = mixed + jnp.where((wide_lane >= second) & (wide_lane < third), strip, 0.0)
    out[:, slots * qa :, :] = mixed.reshape(nc, qa, LANES) + moved[None]


def bump(state, hess, full, drive, rate):
    scale = jnp.sum(jnp.abs(hess), axis=1, keepdims=True) + 1e-06
    push = jnp.dot(hess, full, precision=HIGH, preferred_element_type=jnp.float32)
    return jnp.maximum(state - rate * (push - drive) / scale, 0.0)


def project_kernel(sweep, last, meta, steps, got_c, got_r, at3, ct3, gram_c, b_ref, *refs):
    if last:
        new_a, new_c, new_b, sa = refs
    else:
        send, new_b, sa = refs
    tiles_a, rank, tile = at3.shape
    tiles_c = ct3.shape[0]
    nc, nr = got_c.shape[0], got_r.shape[0]
    slots = meta.shape[1]
    half, qa, qb = rank // LANES, rank // nc, rank // nr
    own = b_ref.shape[0]
    third = LANES // 2
    mine = pl.ds(pl.multiple_of(meta[4, 1] * qa, qa), qa)
    at = own * half
    for h in range(half):
        part = got_r[:, at + h * qb : at + (h + 1) * qb, :]
        sa[:, h * LANES : (h + 1) * LANES] = part.reshape(rank, LANES)
    drive_b = jnp.concatenate(
        [jnp.sum(got_r[:, own * h : own * (h + 1), :], axis=0) for h in range(half)], axis=1
    )
    at += qb * half
    drive_c = [
        jnp.sum(got_r[:, at + t * qa : at + (t + 1) * qa, :], axis=0) for t in range(tiles_c)
    ]
    at += tiles_c * qa
    per = LANES // qb
    sb_parts = []
    for h in range(half):
        part = got_r[h * per, at : at + qa, :]
        for i in range(1, per):
            part = part + pltpu.roll(got_r[h * per + i, at : at + qa, :], qb * i, 1)
        sb_parts.append(part)
    sb_c = jnp.concatenate(sb_parts, axis=1)
    drive_a = [jnp.zeros((qa, tile), jnp.float32) for _ in range(tiles_a)]
    for s in range(nc):
        for m in range(slots):
            value = got_c[s, m * qa : (m + 1) * qa, :]
            spot = got_c[s, slots * qa : (slots + 1) * qa, third + m : third + m + 1]
            spot = jnp.broadcast_to(spot, value.shape)
            for t in range(tiles_a):
                drive_a[t] = drive_a[t] + jnp.where(spot == float(t), value, 0.0)
    hess = sb_c * gram_c[mine, :]
    for t in range(tiles_a):
        new = bump(at3[t, mine, :], hess, at3[t], drive_a[t], steps[sweep, 0])
        if last:
            new_a[t] = new
        else:
            send[:, t * qa : (t + 1) * qa, :] = jnp.broadcast_to(new[None], (nc,) + new.shape)
    hess = sa[mine, :] * sb_c
    for t in range(tiles_c):
        new = bump(ct3[t, mine, :], hess, ct3[t], drive_c[t], steps[sweep, 2])
        if last:
            new_c[t] = new
        else:
            at = (tiles_a + t) * qa
            send[:, at : at + qa, :] = jnp.broadcast_to(new[None], (nc,) + new.shape)
    hess = sa[...] * gram_c[...]
    scale = jnp.sum(jnp.abs(hess), axis=0, keepdims=True) + 1e-06
    old = b_ref[...]
    push = jnp.dot(old, hess, precision=HIGH, preferred_element_type=jnp.float32)
    new_b[...] = jnp.maximum(old - steps[sweep, 1] * (push - drive_b) / scale, 0.0)


def call(kernel, shapes, scratch, flops, moved, operands, scalars=1):
    memory = [pltpu.SMEM] * scalars + [pltpu.VMEM] * (len(operands) - scalars)
    return pl.pallas_call(
        kernel,
        out_shape=[jax.ShapeDtypeStruct(shape, jnp.float32) for shape in shapes],
        in_specs=[pl.BlockSpec(memory_space=m) for m in memory],
        out_specs=[pl.BlockSpec(memory_space=pltpu.VMEM)] * len(shapes),
        scratch_shapes=scratch,
        cost_estimate=pl.CostEstimate(flops=flops, bytes_accessed=moved, transcendentals=0),
        compiler_params=pltpu.CompilerParams(vmem_limit_bytes=32 << 20),
    )(*operands)


def lanes(x):
    return jnp.stack([x[:, t * LANES : (t + 1) * LANES] for t in range(x.shape[1] // LANES)])


def shards(bricks, brick_coords, brick_counts, step_sizes, init_a, init_b, init_c):
    nr, nc = lax.axis_size("row"), lax.axis_size("col")
    row, col = lax.axis_index("row"), lax.axis_index("col")
    slab, places, own = bricks[0, 0], brick_coords[0, 0], brick_counts[0, 0]
    slots, depth, tile, _ = slab.shape
    sweeps = step_sizes.shape[0]
    rank = init_a.shape[-1]
    own_a, own_b = init_a.shape[1], init_b.shape[1]
    tiles_a, tiles_b = own_a * nc // tile, own_b * nr // tile
    length = init_c.shape[0]
    layers, tiles_c = length // depth, length // LANES
    qa, qb = rank // nc, rank // nr
    f32, bf16 = jnp.float32, jnp.bfloat16
    half = rank // LANES

    live = lax.iota(jnp.int32, slots) < own
    meta = jnp.concatenate(
        [
            jnp.where(live[None, :], places, 0),
            live[None, :].astype(jnp.int32),
            jnp.zeros((1, slots), jnp.int32).at[0, 0].set(row).at[0, 1].set(col),
        ],
        axis=0,
    )
    state_b = init_b[0]
    c_bf = init_c.astype(bf16)

    for sweep in range(sweeps):
        b_bf = state_b.astype(bf16)
        if sweep == 0:
            rows = swap(spread(fold(init_a[0]), nc), "col")
            a_rows = unfold(rows, rank).reshape(tiles_a, tile, rank)
            at3 = jnp.swapaxes(a_rows, 1, 2)
            a_bf3 = a_rows.astype(bf16)
            ct3 = lanes(init_c.T)
        else:
            got = swap(send, "col")
            chunk, c_got = take(got, [tiles_a * qa, tiles_c * qa])
            at3 = jnp.swapaxes(chunk.reshape(nc, tiles_a, qa, tile), 0, 1).reshape(tiles_a, rank, tile)
            a_bf3 = jnp.swapaxes(at3.astype(bf16), 1, 2)
            ct3 = jnp.swapaxes(c_got.reshape(nc, tiles_c, qa, LANES), 0, 1).reshape(tiles_c, rank, LANES)
            c_bf = jnp.swapaxes(ct3.astype(bf16), 1, 2).reshape(length, rank)
        a_all = a_bf3.reshape(tiles_a * tile, rank)
        gram_a = gram(a_all)
        slice_a = lax.dynamic_slice_in_dim(gram_a, col * qa, qa, 0)
        slice_a = jnp.swapaxes(slice_a.reshape(qa, nr, qb), 0, 1)
        high = lax.reduce_precision(slice_a, 8, 7)
        pair = pad_lanes(jnp.concatenate([high, slice_a - high], axis=2).astype(bf16))
        send = jnp.concatenate(
            [jnp.broadcast_to(fold(b_bf)[None], (nr, own_b * half, LANES)), fold(pair)], axis=1
        )
        got = swap(send, "row")
        gram_c = gram(c_bf)
        work = 2 * slots * depth * tile * tile * rank
        (blocks,) = call(
            deep_kernel,
            [(nr, own_b * half, LANES)],
            [pltpu.VMEM((tiles_b * tile, rank), f32)],
            work, slab.size * 2, (meta, slab, a_bf3, c_bf),
        )
        (send,) = call(
            wide_kernel,
            [(nc, qa * (slots + 1), LANES)],
            [pltpu.VMEM((tiles_b * tile, rank), bf16), pltpu.VMEM((LANES, rank), f32)],
            work, slab.size * 2, (meta, got, slab, a_bf3, c_bf),
        )
        got_c = swap(send, "col")
        mixed = got_c[:, slots * qa :]
        second = slots * depth + qb
        third = second + qb
        spots_k = mixed[:, 0, third + slots : third + 2 * slots]
        onehot = (spots_k[:, :, None] == lax.iota(jnp.int32, layers).astype(f32)).astype(f32)
        c_got = mixed[:, :, : slots * depth].reshape(nc, qa, slots, depth)
        drive_c = jnp.einsum("sqmk,smb->qbk", c_got, onehot, precision=HIGH).reshape(qa, length)
        strip = mixed[:, :, slots * depth : second].reshape(rank, qb).T
        piece_b = pad_lanes(jnp.sum(mixed[:, :, second:third], axis=0))
        everyone = jnp.concatenate([fold(strip), fold(drive_c), piece_b], axis=0)
        everyone = jnp.broadcast_to(everyone[None], (nr,) + everyone.shape)
        got_r = swap(jnp.concatenate([blocks, everyone], axis=1), "row")
        last = sweep == sweeps - 1
        part_a, part_c = (tiles_a, qa, tile), (tiles_c, qa, LANES)
        shapes = [part_a, part_c] if last else [(nc, (tiles_a + tiles_c) * qa, LANES)]
        results = call(
            functools.partial(project_kernel, sweep, last),
            shapes + [state_b.shape],
            [pltpu.VMEM((rank, rank), f32)],
            12 * rank * rank * tile, 8 * rank * rank * 4,
            (meta, step_sizes, got_c, got_r, at3, ct3, gram_c, state_b), scalars=2,
        )
        if last:
            new_a, new_c, state_b = results
        else:
            send, state_b = results
    per_a = tile // own_a
    own = new_a.reshape(tiles_a, qa, per_a, own_a).transpose(0, 2, 1, 3).reshape(nc, qa, own_a)
    own = fold(pad_lanes(own))
    everyone = jnp.broadcast_to(new_c.reshape(1, -1, LANES), (nc, qa * tiles_c, LANES))
    got = swap(jnp.concatenate([own, everyone], axis=1), "col")
    a_got, c_got = take(got, [own.shape[1], qa * tiles_c])
    out_a = unfold(a_got, own_a + -own_a % LANES)[:, :, :own_a].reshape(rank, own_a).T
    out_c = jnp.swapaxes(c_got.reshape(nc, tiles_c, qa, LANES), 0, 1).reshape(tiles_c, rank, LANES)
    out_c = jnp.swapaxes(out_c, 1, 2).reshape(length, rank)
    return out_a[None], state_b[None], out_c


def solution(mesh):
    placed = (
        P("row", "col", None, None, None, None),
        P("row", "col", None, None),
        P("row", "col"),
        P(),
        P("row", "col", None),
        P("col", "row", None),
        P(),
    )
    return jax.shard_map(
        shards,
        mesh=mesh,
        in_specs=placed,
        out_specs=(P("row", "col", None), P("col", "row", None), P()),
        check_vma=False,
    )
```

```python
import functools

import jax
import jax.numpy as jnp
from jax import lax
from jax.experimental import pallas as pl
from jax.experimental.pallas import tpu as pltpu
from jax.sharding import PartitionSpec as P

LANES = 128
HIGH = lax.Precision.HIGHEST


def swap(x, axis):
    return lax.all_to_all(x, axis, 0, 0, tiled=True)


def chip_gather(x):
    nc = lax.axis_size("col")
    groups = [[chip * 2 + core for chip in range(nc // 2)] for core in range(2)]
    near = lax.all_to_all(x, "col", 0, 0, axis_index_groups=groups, tiled=True)
    far = lax.ppermute(near, "col", [(i, i ^ 1) for i in range(nc)])
    even = lax.axis_index("col") % 2 == 0
    pair = jnp.stack([jnp.where(even, near, far), jnp.where(even, far, near)], axis=1)
    return pair.reshape((nc,) + x.shape[1:])


def spread(x, peers):
    return lax.optimization_barrier(jnp.broadcast_to(x[None], (peers,) + x.shape))


def pad_lanes(x):
    short = -x.shape[-1] % LANES
    return jnp.pad(x, [(0, 0)] * (x.ndim - 1) + [(0, short)])


def fold(x):
    lead, (m, n) = x.shape[:-2], x.shape[-2:]
    parts = [x[..., t * LANES : (t + 1) * LANES] for t in range(n // LANES)]
    return jnp.concatenate(parts, axis=-2)


def unfold(x, n):
    tiles = n // LANES
    m = x.shape[-2] // tiles
    return jnp.concatenate([x[..., t * m : (t + 1) * m, :] for t in range(tiles)], axis=-1)


def take(x, sizes):
    out, at = [], 0
    for size in sizes:
        out.append(x[:, at : at + size])
        at += size
    return out


def gram(values):
    return lax.dot_general(
        values, values, (((0,), (0,)), ((), ())), preferred_element_type=jnp.float32
    )


def deep_kernel(meta, slab, a_ref, c_ref, out, drive):
    slots, depth, tile, _ = slab.shape
    nr, rows, _ = out.shape
    half = a_ref.shape[2] // LANES
    own = rows // half
    drive[...] = jnp.zeros_like(drive)
    for slot in range(slots):
        a_tile = a_ref[meta[0, slot]]
        c_rows = c_ref[pl.ds(pl.multiple_of(meta[2, slot] * depth, depth), depth), :]
        c_rows = c_rows.astype(jnp.float32)
        total = jnp.zeros(a_tile.shape, jnp.float32)
        for k in range(depth):
            deep = lax.dot_general(
                slab[slot, k], a_tile, (((0,), (0,)), ((), ())),
                preferred_element_type=jnp.float32,
            )
            total = total + deep * c_rows[k : k + 1, :]
        spot = pl.ds(pl.multiple_of(meta[1, slot] * tile, tile), tile)
        drive[spot, :] = drive[spot, :] + jnp.where(meta[3, slot] > 0, total, 0.0)
    for h in range(half):
        part = drive[:, h * LANES : (h + 1) * LANES]
        out[:, own * h : own * (h + 1), :] = part.reshape(nr, own, LANES)


def wide_kernel(meta, got, slab, a_ref, c_ref, out, b_all, deep_c):
    slots, depth, tile, _ = slab.shape
    nr = got.shape[0]
    nc = out.shape[0]
    rank = a_ref.shape[2]
    half, qa, qb = rank // LANES, rank // nc, rank // nr
    own = b_all.shape[0] // nr
    for h in range(half):
        part = got[:, own * h : own * (h + 1), :]
        b_all[:, h * LANES : (h + 1) * LANES] = part.reshape(nr * own, LANES)
    deep_c[...] = jnp.zeros_like(deep_c)
    for slot in range(slots):
        b_tile = b_all[pl.ds(pl.multiple_of(meta[1, slot] * tile, tile), tile), :]
        a_tile = a_ref[meta[0, slot]].astype(jnp.float32)
        c_rows = c_ref[pl.ds(pl.multiple_of(meta[2, slot] * depth, depth), depth), :]
        c_rows = c_rows.astype(jnp.float32)
        total = jnp.zeros((tile, rank), jnp.float32)
        for k in range(depth):
            wide = jnp.dot(slab[slot, k], b_tile, preferred_element_type=jnp.float32)
            total = total + wide * c_rows[k : k + 1, :]
            deep_c[slot * depth + k : slot * depth + k + 1, :] = jnp.sum(
                wide * a_tile, axis=0, keepdims=True
            )
        out[:, slot * qa : (slot + 1) * qa, :] = total.T.reshape(nc, qa, LANES)
    whole = b_all[...]
    gram_b = lax.dot_general(
        whole, whole, (((0,), (0,)), ((), ())), preferred_element_type=jnp.float32
    )
    row = meta[4, 0]
    per = LANES // qb
    strip = gram_b[:, :LANES]
    for h in range(1, half):
        strip = jnp.where(row // per == h, gram_b[:, h * LANES : (h + 1) * LANES], strip)
    first = slots * depth
    second = first + qb
    third = second + qb
    strip = pltpu.roll(strip, (second + LANES - qb * (row % per)) % LANES, 1)
    pieces = got[:, own * half : own * half + qa, :].astype(jnp.float32)
    piece = jnp.sum(pieces, axis=0)
    moved = pltpu.roll(piece, first, 1) + pltpu.roll(piece, first - qb, 1)
    lane = lax.broadcasted_iota(jnp.int32, piece.shape, 1)
    spots = jnp.zeros(piece.shape, jnp.int32)
    for m in range(slots):
        alive = meta[3, m] > 0
        spots = jnp.where(lane == third + m, jnp.where(alive, meta[0, m], -1), spots)
        spots = jnp.where(lane == third + slots + m, jnp.where(alive, meta[2, m], -1), spots)
    moved = jnp.where((lane >= first) & (lane < second), moved, spots.astype(jnp.float32))
    wide_lane = lax.broadcasted_iota(jnp.int32, strip.shape, 1)
    mixed = deep_c[...].T
    mixed = mixed + jnp.where((wide_lane >= second) & (wide_lane < third), strip, 0.0)
    out[:, slots * qa :, :] = mixed.reshape(nc, qa, LANES) + moved[None]


def bump(state, hess, full, drive, rate):
    scale = jnp.sum(jnp.abs(hess), axis=1, keepdims=True) + 1e-06
    push = jnp.dot(hess, full, precision=HIGH, preferred_element_type=jnp.float32)
    return jnp.maximum(state - rate * (push - drive) / scale, 0.0)


def project_kernel(sweep, last, meta, steps, got_c, got_r, at3, ct3, gram_c, b_ref, *refs):
    if last:
        new_a, new_c, new_b, sa = refs
    else:
        send, new_b, sa = refs
    tiles_a, rank, tile = at3.shape
    tiles_c = ct3.shape[0]
    nc, nr = got_c.shape[0], got_r.shape[0]
    slots = meta.shape[1]
    half, qa, qb = rank // LANES, rank // nc, rank // nr
    own = b_ref.shape[0]
    third = LANES // 2
    mine = pl.ds(pl.multiple_of(meta[4, 1] * qa, qa), qa)
    at = own * half
    for h in range(half):
        part = got_r[:, at + h * qb : at + (h + 1) * qb, :]
        sa[:, h * LANES : (h + 1) * LANES] = part.reshape(rank, LANES)
    drive_b = jnp.concatenate(
        [jnp.sum(got_r[:, own * h : own * (h + 1), :], axis=0) for h in range(half)], axis=1
    )
    at += qb * half
    drive_c = [
        jnp.sum(got_r[:, at + t * qa : at + (t + 1) * qa, :], axis=0) for t in range(tiles_c)
    ]
    at += tiles_c * qa
    per = LANES // qb
    sb_parts = []
    for h in range(half):
        part = got_r[h * per, at : at + qa, :]
        for i in range(1, per):
            part = part + pltpu.roll(got_r[h * per + i, at : at + qa, :], qb * i, 1)
        sb_parts.append(part)
    sb_c = jnp.concatenate(sb_parts, axis=1)
    drive_a = [jnp.zeros((qa, tile), jnp.float32) for _ in range(tiles_a)]
    for s in range(nc):
        for m in range(slots):
            value = got_c[s, m * qa : (m + 1) * qa, :]
            spot = got_c[s, slots * qa : (slots + 1) * qa, third + m : third + m + 1]
            spot = jnp.broadcast_to(spot, value.shape)
            for t in range(tiles_a):
                drive_a[t] = drive_a[t] + jnp.where(spot == float(t), value, 0.0)
    hess = sb_c * gram_c[mine, :]
    for t in range(tiles_a):
        new = bump(at3[t, mine, :], hess, at3[t], drive_a[t], steps[sweep, 0])
        if last:
            new_a[t] = new
        else:
            send[:, t * qa : (t + 1) * qa, :] = jnp.broadcast_to(new[None], (nc // 2,) + new.shape)
    hess = sa[mine, :] * sb_c
    for t in range(tiles_c):
        new = bump(ct3[t, mine, :], hess, ct3[t], drive_c[t], steps[sweep, 2])
        if last:
            new_c[t] = new
        else:
            at = (tiles_a + t) * qa
            send[:, at : at + qa, :] = jnp.broadcast_to(new[None], (nc // 2,) + new.shape)
    hess = sa[...] * gram_c[...]
    scale = jnp.sum(jnp.abs(hess), axis=0, keepdims=True) + 1e-06
    old = b_ref[...]
    push = jnp.dot(old, hess, precision=HIGH, preferred_element_type=jnp.float32)
    new_b[...] = jnp.maximum(old - steps[sweep, 1] * (push - drive_b) / scale, 0.0)


def call(kernel, shapes, scratch, flops, moved, operands, scalars=1):
    memory = [pltpu.SMEM] * scalars + [pltpu.VMEM] * (len(operands) - scalars)
    return pl.pallas_call(
        kernel,
        out_shape=[jax.ShapeDtypeStruct(shape, jnp.float32) for shape in shapes],
        in_specs=[pl.BlockSpec(memory_space=m) for m in memory],
        out_specs=[pl.BlockSpec(memory_space=pltpu.VMEM)] * len(shapes),
        scratch_shapes=scratch,
        cost_estimate=pl.CostEstimate(flops=flops, bytes_accessed=moved, transcendentals=0),
        compiler_params=pltpu.CompilerParams(vmem_limit_bytes=32 << 20),
    )(*operands)


def lanes(x):
    return jnp.stack([x[:, t * LANES : (t + 1) * LANES] for t in range(x.shape[1] // LANES)])


def shards(bricks, brick_coords, brick_counts, step_sizes, init_a, init_b, init_c):
    nr, nc = lax.axis_size("row"), lax.axis_size("col")
    row, col = lax.axis_index("row"), lax.axis_index("col")
    slab, places, own = bricks[0, 0], brick_coords[0, 0], brick_counts[0, 0]
    slots, depth, tile, _ = slab.shape
    sweeps = step_sizes.shape[0]
    rank = init_a.shape[-1]
    own_a, own_b = init_a.shape[1], init_b.shape[1]
    tiles_a, tiles_b = own_a * nc // tile, own_b * nr // tile
    length = init_c.shape[0]
    layers, tiles_c = length // depth, length // LANES
    qa, qb = rank // nc, rank // nr
    f32, bf16 = jnp.float32, jnp.bfloat16
    half = rank // LANES

    live = lax.iota(jnp.int32, slots) < own
    meta = jnp.concatenate(
        [
            jnp.where(live[None, :], places, 0),
            live[None, :].astype(jnp.int32),
            jnp.zeros((1, slots), jnp.int32).at[0, 0].set(row).at[0, 1].set(col),
        ],
        axis=0,
    )
    state_b = init_b[0]
    c_bf = init_c.astype(bf16)

    for sweep in range(sweeps):
        b_bf = state_b.astype(bf16)
        if sweep == 0:
            rows = swap(spread(fold(init_a[0]), nc), "col")
            a_rows = unfold(rows, rank).reshape(tiles_a, tile, rank)
            at3 = jnp.swapaxes(a_rows, 1, 2)
            a_bf3 = a_rows.astype(bf16)
            ct3 = lanes(init_c.T)
        else:
            got = chip_gather(send)
            chunk, c_got = take(got, [tiles_a * qa, tiles_c * qa])
            at3 = jnp.swapaxes(chunk.reshape(nc, tiles_a, qa, tile), 0, 1).reshape(tiles_a, rank, tile)
            a_bf3 = jnp.swapaxes(at3.astype(bf16), 1, 2)
            ct3 = jnp.swapaxes(c_got.reshape(nc, tiles_c, qa, LANES), 0, 1).reshape(tiles_c, rank, LANES)
            c_bf = jnp.swapaxes(ct3.astype(bf16), 1, 2).reshape(length, rank)
        a_all = a_bf3.reshape(tiles_a * tile, rank)
        gram_a = gram(a_all)
        slice_a = lax.dynamic_slice_in_dim(gram_a, col * qa, qa, 0)
        slice_a = jnp.swapaxes(slice_a.reshape(qa, nr, qb), 0, 1)
        high = lax.reduce_precision(slice_a, 8, 7)
        pair = pad_lanes(jnp.concatenate([high, slice_a - high], axis=2).astype(bf16))
        send = jnp.concatenate(
            [jnp.broadcast_to(fold(b_bf)[None], (nr, own_b * half, LANES)), fold(pair)], axis=1
        )
        got = swap(send, "row")
        gram_c = gram(c_bf)
        work = 2 * slots * depth * tile * tile * rank
        (blocks,) = call(
            deep_kernel,
            [(nr, own_b * half, LANES)],
            [pltpu.VMEM((tiles_b * tile, rank), f32)],
            work, slab.size * 2, (meta, slab, a_bf3, c_bf),
        )
        (send,) = call(
            wide_kernel,
            [(nc, qa * (slots + 1), LANES)],
            [pltpu.VMEM((tiles_b * tile, rank), bf16), pltpu.VMEM((LANES, rank), f32)],
            work, slab.size * 2, (meta, got, slab, a_bf3, c_bf),
        )
        got_c = swap(send, "col")
        mixed = got_c[:, slots * qa :]
        second = slots * depth + qb
        third = second + qb
        spots_k = mixed[:, 0, third + slots : third + 2 * slots]
        onehot = (spots_k[:, :, None] == lax.iota(jnp.int32, layers).astype(f32)).astype(f32)
        c_got = mixed[:, :, : slots * depth].reshape(nc, qa, slots, depth)
        drive_c = jnp.einsum("sqmk,smb->qbk", c_got, onehot, precision=HIGH).reshape(qa, length)
        strip = mixed[:, :, slots * depth : second].reshape(rank, qb).T
        piece_b = pad_lanes(jnp.sum(mixed[:, :, second:third], axis=0))
        everyone = jnp.concatenate([fold(strip), fold(drive_c), piece_b], axis=0)
        everyone = jnp.broadcast_to(everyone[None], (nr,) + everyone.shape)
        got_r = swap(jnp.concatenate([blocks, everyone], axis=1), "row")
        last = sweep == sweeps - 1
        part_a, part_c = (tiles_a, qa, tile), (tiles_c, qa, LANES)
        shapes = [part_a, part_c] if last else [(nc // 2, (tiles_a + tiles_c) * qa, LANES)]
        results = call(
            functools.partial(project_kernel, sweep, last),
            shapes + [state_b.shape],
            [pltpu.VMEM((rank, rank), f32)],
            12 * rank * rank * tile, 8 * rank * rank * 4,
            (meta, step_sizes, got_c, got_r, at3, ct3, gram_c, state_b), scalars=2,
        )
        if last:
            new_a, new_c, state_b = results
        else:
            send, state_b = results
    per_a = tile // own_a
    own = new_a.reshape(tiles_a, qa, per_a, own_a).transpose(0, 2, 1, 3).reshape(nc, qa, own_a)
    own = fold(pad_lanes(own))
    everyone = jnp.broadcast_to(new_c.reshape(1, -1, LANES), (nc, qa * tiles_c, LANES))
    got = swap(jnp.concatenate([own, everyone], axis=1), "col")
    a_got, c_got = take(got, [own.shape[1], qa * tiles_c])
    out_a = unfold(a_got, own_a + -own_a % LANES)[:, :, :own_a].reshape(rank, own_a).T
    out_c = jnp.swapaxes(c_got.reshape(nc, tiles_c, qa, LANES), 0, 1).reshape(tiles_c, rank, LANES)
    out_c = jnp.swapaxes(out_c, 1, 2).reshape(length, rank)
    return out_a[None], state_b[None], out_c


def solution(mesh):
    placed = (
        P("row", "col", None, None, None, None),
        P("row", "col", None, None),
        P("row", "col"),
        P(),
        P("row", "col", None),
        P("col", "row", None),
        P(),
    )
    return jax.shard_map(
        shards,
        mesh=mesh,
        in_specs=placed,
        out_specs=(P("row", "col", None), P("col", "row", None), P()),
        check_vma=False,
    )
```

```python
import functools

import jax
import jax.numpy as jnp
from jax import lax
from jax.experimental import pallas as pl
from jax.experimental.pallas import tpu as pltpu
from jax.sharding import PartitionSpec as P

LANES = 128
HIGH = lax.Precision.HIGHEST


def swap(x, axis):
    return lax.all_to_all(x, axis, 0, 0, tiled=True)


def chip_gather(x):
    nc = lax.axis_size("col")
    groups = [[chip * 2 + core for chip in range(nc // 2)] for core in range(2)]
    near = lax.all_to_all(x, "col", 0, 0, axis_index_groups=groups, tiled=True)
    far = lax.ppermute(near, "col", [(i, i ^ 1) for i in range(nc)])
    even = lax.axis_index("col") % 2 == 0
    pair = jnp.stack([jnp.where(even, near, far), jnp.where(even, far, near)], axis=1)
    return pair.reshape((nc,) + x.shape[1:])


def spread(x, peers):
    return lax.optimization_barrier(jnp.broadcast_to(x[None], (peers,) + x.shape))


def pad_lanes(x):
    short = -x.shape[-1] % LANES
    return jnp.pad(x, [(0, 0)] * (x.ndim - 1) + [(0, short)])


def fold(x):
    lead, (m, n) = x.shape[:-2], x.shape[-2:]
    parts = [x[..., t * LANES : (t + 1) * LANES] for t in range(n // LANES)]
    return jnp.concatenate(parts, axis=-2)


def unfold(x, n):
    tiles = n // LANES
    m = x.shape[-2] // tiles
    return jnp.concatenate([x[..., t * m : (t + 1) * m, :] for t in range(tiles)], axis=-1)


def take(x, sizes):
    out, at = [], 0
    for size in sizes:
        out.append(x[:, at : at + size])
        at += size
    return out


def gram(values):
    return lax.dot_general(
        values, values, (((0,), (0,)), ((), ())), preferred_element_type=jnp.float32
    )


def deep_kernel(meta, slab, a_ref, c_ref, out, drive):
    slots, depth, tile, _ = slab.shape
    nr, rows, _ = out.shape
    half = a_ref.shape[2] // LANES
    own = rows // half
    drive[...] = jnp.zeros_like(drive)
    for slot in range(slots):
        a_tile = a_ref[meta[0, slot]]
        c_rows = c_ref[pl.ds(pl.multiple_of(meta[2, slot] * depth, depth), depth), :]
        c_rows = c_rows.astype(jnp.float32)
        total = jnp.zeros(a_tile.shape, jnp.float32)
        for k in range(depth):
            deep = lax.dot_general(
                slab[slot, k], a_tile, (((0,), (0,)), ((), ())),
                preferred_element_type=jnp.float32,
            )
            total = total + deep * c_rows[k : k + 1, :]
        spot = pl.ds(pl.multiple_of(meta[1, slot] * tile, tile), tile)
        drive[spot, :] = drive[spot, :] + jnp.where(meta[3, slot] > 0, total, 0.0)
    for h in range(half):
        part = drive[:, h * LANES : (h + 1) * LANES]
        out[:, own * h : own * (h + 1), :] = part.reshape(nr, own, LANES)


def wide_kernel(meta, got, slab, a_ref, c_ref, out, b_all, deep_c):
    slots, depth, tile, _ = slab.shape
    nr = got.shape[0]
    nc = out.shape[0]
    rank = a_ref.shape[2]
    half, qa, qb = rank // LANES, rank // nc, rank // nr
    own = b_all.shape[0] // nr
    for h in range(half):
        part = got[:, own * h : own * (h + 1), :]
        b_all[:, h * LANES : (h + 1) * LANES] = part.reshape(nr * own, LANES)
    deep_c[...] = jnp.zeros_like(deep_c)
    for slot in range(slots):
        b_tile = b_all[pl.ds(pl.multiple_of(meta[1, slot] * tile, tile), tile), :]
        a_tile = a_ref[meta[0, slot]].astype(jnp.float32)
        c_rows = c_ref[pl.ds(pl.multiple_of(meta[2, slot] * depth, depth), depth), :]
        c_rows = c_rows.astype(jnp.float32)
        total = jnp.zeros((tile, rank), jnp.float32)
        for k in range(depth):
            wide = jnp.dot(slab[slot, k], b_tile, preferred_element_type=jnp.float32)
            total = total + wide * c_rows[k : k + 1, :]
            deep_c[slot * depth + k : slot * depth + k + 1, :] = jnp.sum(
                wide * a_tile, axis=0, keepdims=True
            )
        out[:, slot * qa : (slot + 1) * qa, :] = total.T.reshape(nc, qa, LANES)
    whole = b_all[...]
    gram_b = lax.dot_general(
        whole, whole, (((0,), (0,)), ((), ())), preferred_element_type=jnp.float32
    )
    row = meta[4, 0]
    per = LANES // qb
    strip = gram_b[:, :LANES]
    for h in range(1, half):
        strip = jnp.where(row // per == h, gram_b[:, h * LANES : (h + 1) * LANES], strip)
    first = slots * depth
    second = first + qb
    third = second + qb
    strip = pltpu.roll(strip, (second + LANES - qb * (row % per)) % LANES, 1)
    pieces = got[:, own * half : own * half + qa, :].astype(jnp.float32)
    piece = jnp.sum(pieces, axis=0)
    moved = pltpu.roll(piece, first, 1) + pltpu.roll(piece, first - qb, 1)
    lane = lax.broadcasted_iota(jnp.int32, piece.shape, 1)
    spots = jnp.zeros(piece.shape, jnp.int32)
    for m in range(slots):
        alive = meta[3, m] > 0
        spots = jnp.where(lane == third + m, jnp.where(alive, meta[0, m], -1), spots)
        spots = jnp.where(lane == third + slots + m, jnp.where(alive, meta[2, m], -1), spots)
    moved = jnp.where((lane >= first) & (lane < second), moved, spots.astype(jnp.float32))
    wide_lane = lax.broadcasted_iota(jnp.int32, strip.shape, 1)
    mixed = deep_c[...].T
    mixed = mixed + jnp.where((wide_lane >= second) & (wide_lane < third), strip, 0.0)
    out[:, slots * qa :, :] = mixed.reshape(nc, qa, LANES) + moved[None]


def bump(state, hess, full, drive, rate):
    scale = jnp.sum(jnp.abs(hess), axis=1, keepdims=True) + 1e-06
    push = jnp.dot(hess, full, precision=HIGH, preferred_element_type=jnp.float32)
    return jnp.maximum(state - rate * (push - drive) / scale, 0.0)


def project_kernel(sweep, last, meta, steps, got_c, got_r, at3, ct3, gram_c, b_ref, *refs):
    if last:
        new_a, new_c, new_b, sa = refs
    else:
        send, new_b, sa = refs
    tiles_a, rank, tile = at3.shape
    tiles_c = ct3.shape[0]
    nc, nr = got_c.shape[0], got_r.shape[0]
    slots = meta.shape[1]
    half, qa, qb = rank // LANES, rank // nc, rank // nr
    own = b_ref.shape[0]
    third = LANES // 2
    mine = pl.ds(pl.multiple_of(meta[4, 1] * qa, qa), qa)
    at = own * half
    for h in range(half):
        part = got_r[:, at + h * qb : at + (h + 1) * qb, :]
        sa[:, h * LANES : (h + 1) * LANES] = part.reshape(rank, LANES)
    drive_b = jnp.concatenate(
        [jnp.sum(got_r[:, own * h : own * (h + 1), :], axis=0) for h in range(half)], axis=1
    )
    at += qb * half
    drive_c = [
        jnp.sum(got_r[:, at + t * qa : at + (t + 1) * qa, :], axis=0) for t in range(tiles_c)
    ]
    at += tiles_c * qa
    per = LANES // qb
    sb_parts = []
    for h in range(half):
        part = got_r[h * per, at : at + qa, :]
        for i in range(1, per):
            part = part + pltpu.roll(got_r[h * per + i, at : at + qa, :], qb * i, 1)
        sb_parts.append(part)
    sb_c = jnp.concatenate(sb_parts, axis=1)
    drive_a = [jnp.zeros((qa, tile), jnp.float32) for _ in range(tiles_a)]
    for s in range(nc):
        for m in range(slots):
            value = got_c[s, m * qa : (m + 1) * qa, :]
            spot = got_c[s, slots * qa : (slots + 1) * qa, third + m : third + m + 1]
            spot = jnp.broadcast_to(spot, value.shape)
            for t in range(tiles_a):
                drive_a[t] = drive_a[t] + jnp.where(spot == float(t), value, 0.0)
    hess = sb_c * gram_c[mine, :]
    for t in range(tiles_a):
        new = bump(at3[t, mine, :], hess, at3[t], drive_a[t], steps[sweep, 0])
        if last:
            new_a[t] = new
        else:
            send[:, t * qa : (t + 1) * qa, :] = jnp.broadcast_to(new[None], (nc // 2,) + new.shape)
    hess = sa[mine, :] * sb_c
    for t in range(tiles_c):
        new = bump(ct3[t, mine, :], hess, ct3[t], drive_c[t], steps[sweep, 2])
        if last:
            new_c[t] = new
        else:
            at = (tiles_a + t) * qa
            send[:, at : at + qa, :] = jnp.broadcast_to(new[None], (nc // 2,) + new.shape)
    hess = sa[...] * gram_c[...]
    scale = jnp.sum(jnp.abs(hess), axis=0, keepdims=True) + 1e-06
    old = b_ref[...]
    push = jnp.dot(old, hess, precision=HIGH, preferred_element_type=jnp.float32)
    new_b[...] = jnp.maximum(old - steps[sweep, 1] * (push - drive_b) / scale, 0.0)


def call(kernel, shapes, scratch, flops, moved, operands, scalars=1):
    memory = [pltpu.SMEM] * scalars + [pltpu.VMEM] * (len(operands) - scalars)
    return pl.pallas_call(
        kernel,
        out_shape=[jax.ShapeDtypeStruct(shape, jnp.float32) for shape in shapes],
        in_specs=[pl.BlockSpec(memory_space=m) for m in memory],
        out_specs=[pl.BlockSpec(memory_space=pltpu.VMEM)] * len(shapes),
        scratch_shapes=scratch,
        cost_estimate=pl.CostEstimate(flops=flops, bytes_accessed=moved, transcendentals=0),
        compiler_params=pltpu.CompilerParams(vmem_limit_bytes=32 << 20),
    )(*operands)


def lanes(x):
    return jnp.stack([x[:, t * LANES : (t + 1) * LANES] for t in range(x.shape[1] // LANES)])


def shards(bricks, brick_coords, brick_counts, step_sizes, init_a, init_b, init_c):
    nr, nc = lax.axis_size("row"), lax.axis_size("col")
    row, col = lax.axis_index("row"), lax.axis_index("col")
    slab, places, own = bricks[0, 0], brick_coords[0, 0], brick_counts[0, 0]
    slots, depth, tile, _ = slab.shape
    sweeps = step_sizes.shape[0]
    rank = init_a.shape[-1]
    own_a, own_b = init_a.shape[1], init_b.shape[1]
    tiles_a, tiles_b = own_a * nc // tile, own_b * nr // tile
    length = init_c.shape[0]
    layers, tiles_c = length // depth, length // LANES
    qa, qb = rank // nc, rank // nr
    f32, bf16 = jnp.float32, jnp.bfloat16
    half = rank // LANES

    live = lax.iota(jnp.int32, slots) < own
    meta = jnp.concatenate(
        [
            jnp.where(live[None, :], places, 0),
            live[None, :].astype(jnp.int32),
            jnp.zeros((1, slots), jnp.int32).at[0, 0].set(row).at[0, 1].set(col),
        ],
        axis=0,
    )
    state_b = init_b[0]
    c_bf = init_c.astype(bf16)

    for sweep in range(sweeps):
        b_bf = state_b.astype(bf16)
        if sweep == 0:
            rows = chip_gather(spread(fold(init_a[0]), nc // 2))
            a_rows = unfold(rows, rank).reshape(tiles_a, tile, rank)
            at3 = jnp.swapaxes(a_rows, 1, 2)
            a_bf3 = a_rows.astype(bf16)
            ct3 = lanes(init_c.T)
        else:
            got = chip_gather(send)
            chunk, c_got = take(got, [tiles_a * qa, tiles_c * qa])
            at3 = jnp.swapaxes(chunk.reshape(nc, tiles_a, qa, tile), 0, 1).reshape(tiles_a, rank, tile)
            a_bf3 = jnp.swapaxes(at3.astype(bf16), 1, 2)
            ct3 = jnp.swapaxes(c_got.reshape(nc, tiles_c, qa, LANES), 0, 1).reshape(tiles_c, rank, LANES)
            c_bf = jnp.swapaxes(ct3.astype(bf16), 1, 2).reshape(length, rank)
        a_all = a_bf3.reshape(tiles_a * tile, rank)
        gram_a = gram(a_all)
        slice_a = lax.dynamic_slice_in_dim(gram_a, col * qa, qa, 0)
        slice_a = jnp.swapaxes(slice_a.reshape(qa, nr, qb), 0, 1)
        high = lax.reduce_precision(slice_a, 8, 7)
        pair = pad_lanes(jnp.concatenate([high, slice_a - high], axis=2).astype(bf16))
        send = jnp.concatenate(
            [jnp.broadcast_to(fold(b_bf)[None], (nr, own_b * half, LANES)), fold(pair)], axis=1
        )
        got = swap(send, "row")
        gram_c = gram(c_bf)
        work = 2 * slots * depth * tile * tile * rank
        (blocks,) = call(
            deep_kernel,
            [(nr, own_b * half, LANES)],
            [pltpu.VMEM((tiles_b * tile, rank), f32)],
            work, slab.size * 2, (meta, slab, a_bf3, c_bf),
        )
        (send,) = call(
            wide_kernel,
            [(nc, qa * (slots + 1), LANES)],
            [pltpu.VMEM((tiles_b * tile, rank), bf16), pltpu.VMEM((LANES, rank), f32)],
            work, slab.size * 2, (meta, got, slab, a_bf3, c_bf),
        )
        got_c = swap(send, "col")
        mixed = got_c[:, slots * qa :]
        second = slots * depth + qb
        third = second + qb
        spots_k = mixed[:, 0, third + slots : third + 2 * slots]
        onehot = (spots_k[:, :, None] == lax.iota(jnp.int32, layers).astype(f32)).astype(f32)
        c_got = mixed[:, :, : slots * depth].reshape(nc, qa, slots, depth)
        drive_c = jnp.einsum("sqmk,smb->qbk", c_got, onehot, precision=HIGH).reshape(qa, length)
        strip = mixed[:, :, slots * depth : second].reshape(rank, qb).T
        piece_b = pad_lanes(jnp.sum(mixed[:, :, second:third], axis=0))
        everyone = jnp.concatenate([fold(strip), fold(drive_c), piece_b], axis=0)
        everyone = jnp.broadcast_to(everyone[None], (nr,) + everyone.shape)
        got_r = swap(jnp.concatenate([blocks, everyone], axis=1), "row")
        last = sweep == sweeps - 1
        part_a, part_c = (tiles_a, qa, tile), (tiles_c, qa, LANES)
        shapes = [part_a, part_c] if last else [(nc // 2, (tiles_a + tiles_c) * qa, LANES)]
        results = call(
            functools.partial(project_kernel, sweep, last),
            shapes + [state_b.shape],
            [pltpu.VMEM((rank, rank), f32)],
            12 * rank * rank * tile, 8 * rank * rank * 4,
            (meta, step_sizes, got_c, got_r, at3, ct3, gram_c, state_b), scalars=2,
        )
        if last:
            new_a, new_c, state_b = results
        else:
            send, state_b = results
    per_a = tile // own_a
    own = new_a.reshape(tiles_a, qa, per_a, own_a).transpose(0, 2, 1, 3)
    own = own.reshape(nc // 2, 2, qa, own_a).swapaxes(1, 2).reshape(nc // 2, qa, 2 * own_a)
    own = fold(pad_lanes(own))
    everyone = jnp.broadcast_to(new_c.reshape(1, -1, LANES), (nc // 2, qa * tiles_c, LANES))
    got = chip_gather(jnp.concatenate([own, everyone], axis=1))
    a_got, c_got = take(got, [own.shape[1], qa * tiles_c])
    a_got = unfold(a_got, 2 * own_a + -2 * own_a % LANES)
    a_got = jnp.where(col % 2 == 0, a_got[:, :, :own_a], a_got[:, :, own_a : 2 * own_a])
    out_a = a_got.reshape(rank, own_a).T
    out_c = jnp.swapaxes(c_got.reshape(nc, tiles_c, qa, LANES), 0, 1).reshape(tiles_c, rank, LANES)
    out_c = jnp.swapaxes(out_c, 1, 2).reshape(length, rank)
    return out_a[None], state_b[None], out_c


def solution(mesh):
    placed = (
        P("row", "col", None, None, None, None),
        P("row", "col", None, None),
        P("row", "col"),
        P(),
        P("row", "col", None),
        P("col", "row", None),
        P(),
    )
    return jax.shard_map(
        shards,
        mesh=mesh,
        in_specs=placed,
        out_specs=(P("row", "col", None), P("col", "row", None), P()),
        check_vma=False,
    )
```

```python
import functools

import jax
import jax.numpy as jnp
from jax import lax
from jax.experimental import pallas as pl
from jax.experimental.pallas import tpu as pltpu
from jax.sharding import PartitionSpec as P

LANES = 128
HIGH = lax.Precision.HIGHEST


def swap(x, axis):
    return lax.all_to_all(x, axis, 0, 0, tiled=True)


def chip_gather(x):
    nc = lax.axis_size("col")
    groups = [[chip * 2 + core for chip in range(nc // 2)] for core in range(2)]
    near = lax.all_to_all(x, "col", 0, 0, axis_index_groups=groups, tiled=True)
    far = lax.ppermute(near, "col", [(i, i ^ 1) for i in range(nc)])
    even = lax.axis_index("col") % 2 == 0
    pair = jnp.stack([jnp.where(even, near, far), jnp.where(even, far, near)], axis=1)
    return pair.reshape((nc,) + x.shape[1:])


def spread(x, peers):
    return lax.optimization_barrier(jnp.broadcast_to(x[None], (peers,) + x.shape))


def pad_lanes(x):
    short = -x.shape[-1] % LANES
    return jnp.pad(x, [(0, 0)] * (x.ndim - 1) + [(0, short)])


def fold(x):
    lead, (m, n) = x.shape[:-2], x.shape[-2:]
    parts = [x[..., t * LANES : (t + 1) * LANES] for t in range(n // LANES)]
    return jnp.concatenate(parts, axis=-2)


def unfold(x, n):
    tiles = n // LANES
    m = x.shape[-2] // tiles
    return jnp.concatenate([x[..., t * m : (t + 1) * m, :] for t in range(tiles)], axis=-1)


def take(x, sizes):
    out, at = [], 0
    for size in sizes:
        out.append(x[:, at : at + size])
        at += size
    return out


def gram(values):
    return lax.dot_general(
        values, values, (((0,), (0,)), ((), ())), preferred_element_type=jnp.float32
    )


def deep_kernel(meta, steps, slab, a_ref, c_ref, out, drive):
    slots, depth, tile, _ = slab.shape
    nr, rows, _ = out.shape
    half = a_ref.shape[2] // LANES
    own = rows // half
    drive[...] = jnp.zeros_like(drive)
    for slot in range(slots):
        a_tile = a_ref[meta[0, slot]]
        c_rows = c_ref[pl.ds(pl.multiple_of(meta[2, slot] * depth, depth), depth), :]
        c_rows = c_rows.astype(jnp.float32)
        total = jnp.zeros(a_tile.shape, jnp.float32)
        for k in range(depth):
            deep = lax.dot_general(
                slab[slot, k], a_tile, (((0,), (0,)), ((), ())),
                preferred_element_type=jnp.float32,
            )
            total = total + deep * c_rows[k : k + 1, :]
        spot = pl.ds(pl.multiple_of(meta[1, slot] * tile, tile), tile)
        drive[spot, :] = drive[spot, :] + jnp.where(meta[3, slot] > 0, total, 0.0)
    for h in range(half):
        part = drive[:, h * LANES : (h + 1) * LANES]
        out[:, own * h : own * (h + 1), :] = part.reshape(nr, own, LANES)


def wide_kernel(meta, got, slab, a_ref, c_ref, out, b_all, deep_c):
    slots, depth, tile, _ = slab.shape
    nr = got.shape[0]
    nc = out.shape[0]
    rank = a_ref.shape[2]
    half, qa, qb = rank // LANES, rank // nc, rank // nr
    own = b_all.shape[0] // nr
    for h in range(half):
        part = got[:, own * h : own * (h + 1), :]
        b_all[:, h * LANES : (h + 1) * LANES] = part.reshape(nr * own, LANES)
    deep_c[...] = jnp.zeros_like(deep_c)
    for slot in range(slots):
        b_tile = b_all[pl.ds(pl.multiple_of(meta[1, slot] * tile, tile), tile), :]
        a_tile = a_ref[meta[0, slot]].astype(jnp.float32)
        c_rows = c_ref[pl.ds(pl.multiple_of(meta[2, slot] * depth, depth), depth), :]
        c_rows = c_rows.astype(jnp.float32)
        total = jnp.zeros((tile, rank), jnp.float32)
        for k in range(depth):
            wide = jnp.dot(slab[slot, k], b_tile, preferred_element_type=jnp.float32)
            total = total + wide * c_rows[k : k + 1, :]
            deep_c[slot * depth + k : slot * depth + k + 1, :] = jnp.sum(
                wide * a_tile, axis=0, keepdims=True
            )
        out[:, slot * qa : (slot + 1) * qa, :] = total.T.reshape(nc, qa, LANES)
    whole = b_all[...]
    gram_b = lax.dot_general(
        whole, whole, (((0,), (0,)), ((), ())), preferred_element_type=jnp.float32
    )
    row = meta[4, 0]
    per = LANES // qb
    strip = gram_b[:, :LANES]
    for h in range(1, half):
        strip = jnp.where(row // per == h, gram_b[:, h * LANES : (h + 1) * LANES], strip)
    first = slots * depth
    second = first + qb
    third = second + qb
    strip = pltpu.roll(strip, (second + LANES - qb * (row % per)) % LANES, 1)
    pieces = got[:, own * half : own * half + qa, :].astype(jnp.float32)
    piece = jnp.sum(pieces, axis=0)
    moved = pltpu.roll(piece, first, 1) + pltpu.roll(piece, first - qb, 1)
    lane = lax.broadcasted_iota(jnp.int32, piece.shape, 1)
    spots = jnp.zeros(piece.shape, jnp.int32)
    for m in range(slots):
        alive = meta[3, m] > 0
        spots = jnp.where(lane == third + m, jnp.where(alive, meta[0, m], -1), spots)
        spots = jnp.where(lane == third + slots + m, jnp.where(alive, meta[2, m], -1), spots)
    moved = jnp.where((lane >= first) & (lane < second), moved, spots.astype(jnp.float32))
    wide_lane = lax.broadcasted_iota(jnp.int32, strip.shape, 1)
    mixed = deep_c[...].T
    mixed = mixed + jnp.where((wide_lane >= second) & (wide_lane < third), strip, 0.0)
    out[:, slots * qa :, :] = mixed.reshape(nc, qa, LANES) + moved[None]


def bump(state, hess, full, drive, rate):
    scale = jnp.sum(jnp.abs(hess), axis=1, keepdims=True) + 1e-06
    push = jnp.dot(hess, full, precision=HIGH, preferred_element_type=jnp.float32)
    return jnp.maximum(state - rate * (push - drive) / scale, 0.0)


def project_kernel(sweep, last, meta, steps, got_c, got_r, at3, ct3, gram_c, b_ref, *refs):
    if last:
        new_a, new_c, new_b, sa = refs
    else:
        send, new_b, sa = refs
    tiles_a, rank, tile = at3.shape
    tiles_c = ct3.shape[0]
    nc, nr = got_c.shape[0], got_r.shape[0]
    slots = meta.shape[1]
    half, qa, qb = rank // LANES, rank // nc, rank // nr
    own = b_ref.shape[0]
    third = LANES // 2
    mine = pl.ds(pl.multiple_of(meta[4, 1] * qa, qa), qa)
    at = own * half
    tail = at + qb + tiles_c * qa
    lane = lax.broadcasted_iota(jnp.int32, (qb, LANES), 1)
    for r in range(nr):
        rest = got_r[r, tail : tail + qb // 2, :]
        rest = jnp.concatenate(
            [pltpu.roll(rest, LANES - qb, 1), pltpu.roll(rest, LANES - 2 * qb, 1)], axis=0
        )
        parts = [got_r[r, at : at + qb, :], jnp.where(lane < qb, rest, 0.0)]
        whole, shift = divmod(r * qb, LANES)
        if shift:
            turned = [pltpu.roll(part, shift, 1) for part in parts]
            parts = [jnp.where(lane < shift, turned[1 - h], turned[h]) for h in range(2)]
        for h in range(2):
            slot = (h + whole) % 2
            sa[r * qb : (r + 1) * qb, slot * LANES : (slot + 1) * LANES] = parts[h]
    upper = sa[...]
    sa[...] = upper + upper.T
    drive_b = jnp.concatenate(
        [jnp.sum(got_r[:, own * h : own * (h + 1), :], axis=0) for h in range(half)], axis=1
    )
    at += qb
    drive_c = [
        jnp.sum(got_r[:, at + t * qa : at + (t + 1) * qa, :], axis=0) for t in range(tiles_c)
    ]
    at += tiles_c * qa
    per = LANES // qb
    sb_parts = []
    for h in range(half):
        part = jnp.zeros((qa, LANES), jnp.float32)
        for i in range(per):
            piece = got_r[h * per + i, at : at + qa, :]
            piece = jnp.where(lax.broadcasted_iota(jnp.int32, piece.shape, 1) < qb, piece, 0.0)
            part = part + (pltpu.roll(piece, qb * i, 1) if i else piece)
        sb_parts.append(part)
    sb_c = jnp.concatenate(sb_parts, axis=1)
    drive_a = [jnp.zeros((qa, tile), jnp.float32) for _ in range(tiles_a)]
    for s in range(nc):
        for m in range(slots):
            value = got_c[s, m * qa : (m + 1) * qa, :]
            spot = got_c[s, slots * qa : (slots + 1) * qa, third + m : third + m + 1]
            spot = jnp.broadcast_to(spot, value.shape)
            for t in range(tiles_a):
                drive_a[t] = drive_a[t] + jnp.where(spot == float(t), value, 0.0)
    hess = sb_c * gram_c[mine, :]
    for t in range(tiles_a):
        new = bump(at3[t, mine, :], hess, at3[t], drive_a[t], steps[sweep, 0])
        if last:
            new_a[t] = new
        else:
            send[:, t * qa : (t + 1) * qa, :] = jnp.broadcast_to(new[None], (nc // 2,) + new.shape)
    hess = sa[mine, :] * sb_c
    for t in range(tiles_c):
        new = bump(ct3[t, mine, :], hess, ct3[t], drive_c[t], steps[sweep, 2])
        if last:
            new_c[t] = new
        else:
            at = (tiles_a + t) * qa
            send[:, at : at + qa, :] = jnp.broadcast_to(new[None], (nc // 2,) + new.shape)
    hess = sa[...] * gram_c[...]
    scale = jnp.sum(jnp.abs(hess), axis=0, keepdims=True) + 1e-06
    old = b_ref[...]
    push = jnp.dot(old, hess, precision=HIGH, preferred_element_type=jnp.float32)
    new_b[...] = jnp.maximum(old - steps[sweep, 1] * (push - drive_b) / scale, 0.0)


def call(kernel, shapes, scratch, flops, moved, operands, scalars=1):
    memory = [pltpu.SMEM] * scalars + [pltpu.VMEM] * (len(operands) - scalars)
    return pl.pallas_call(
        kernel,
        out_shape=[jax.ShapeDtypeStruct(shape, jnp.float32) for shape in shapes],
        in_specs=[pl.BlockSpec(memory_space=m) for m in memory],
        out_specs=[pl.BlockSpec(memory_space=pltpu.VMEM)] * len(shapes),
        scratch_shapes=scratch,
        cost_estimate=pl.CostEstimate(flops=flops, bytes_accessed=moved, transcendentals=0),
        compiler_params=pltpu.CompilerParams(vmem_limit_bytes=32 << 20),
    )(*operands)


def lanes(x):
    return jnp.stack([x[:, t * LANES : (t + 1) * LANES] for t in range(x.shape[1] // LANES)])


def shards(bricks, brick_coords, brick_counts, step_sizes, init_a, init_b, init_c):
    nr, nc = lax.axis_size("row"), lax.axis_size("col")
    row, col = lax.axis_index("row"), lax.axis_index("col")
    slab, places, own = bricks[0, 0], brick_coords[0, 0], brick_counts[0, 0]
    slots, depth, tile, _ = slab.shape
    sweeps = step_sizes.shape[0]
    rank = init_a.shape[-1]
    own_a, own_b = init_a.shape[1], init_b.shape[1]
    tiles_a, tiles_b = own_a * nc // tile, own_b * nr // tile
    length = init_c.shape[0]
    layers, tiles_c = length // depth, length // LANES
    qa, qb = rank // nc, rank // nr
    f32, bf16 = jnp.float32, jnp.bfloat16
    half = rank // LANES

    live = lax.iota(jnp.int32, slots) < own
    meta = jnp.concatenate(
        [
            jnp.where(live[None, :], places, 0),
            live[None, :].astype(jnp.int32),
            jnp.zeros((1, slots), jnp.int32).at[0, 0].set(row).at[0, 1].set(col),
        ],
        axis=0,
    )
    state_b = init_b[0]
    c_bf = init_c.astype(bf16)

    for sweep in range(sweeps):
        b_bf = state_b.astype(bf16)
        if sweep == 0:
            rows = chip_gather(spread(fold(init_a[0]), nc // 2))
            a_rows = unfold(rows, rank).reshape(tiles_a, tile, rank)
            at3 = jnp.swapaxes(a_rows, 1, 2)
            a_bf3 = a_rows.astype(bf16)
            ct3 = lanes(init_c.T)
        else:
            got = chip_gather(send)
            chunk, c_got = take(got, [tiles_a * qa, tiles_c * qa])
            at3 = jnp.swapaxes(chunk.reshape(nc, tiles_a, qa, tile), 0, 1).reshape(tiles_a, rank, tile)
            a_bf3 = jnp.swapaxes(at3.astype(bf16), 1, 2)
            ct3 = jnp.swapaxes(c_got.reshape(nc, tiles_c, qa, LANES), 0, 1).reshape(tiles_c, rank, LANES)
            c_bf = jnp.swapaxes(ct3.astype(bf16), 1, 2).reshape(length, rank)
        a_all = a_bf3.reshape(tiles_a * tile, rank)
        gram_a = gram(a_all)
        if sweep == 0:
            a_bf3, at3, ct3 = lax.optimization_barrier((a_bf3, at3, ct3))
        slice_a = lax.dynamic_slice_in_dim(gram_a, col * qa, qa, 0)
        slice_a = jnp.swapaxes(slice_a.reshape(qa, nr, qb), 0, 1)
        high = lax.reduce_precision(slice_a, 8, 7)
        pair = pad_lanes(jnp.concatenate([high, slice_a - high], axis=2).astype(bf16))
        send = jnp.concatenate(
            [jnp.broadcast_to(fold(b_bf)[None], (nr, own_b * half, LANES)), fold(pair)], axis=1
        )
        got = swap(send, "row")
        gram_c = gram(c_bf)
        work = 2 * slots * depth * tile * tile * rank
        (blocks,) = call(
            deep_kernel,
            [(nr, own_b * half, LANES)],
            [pltpu.VMEM((tiles_b * tile, rank), f32)],
            work, slab.size * 2, (meta, step_sizes, slab, a_bf3, c_bf), scalars=2,
        )
        (send,) = call(
            wide_kernel,
            [(nc, qa * (slots + 1), LANES)],
            [pltpu.VMEM((tiles_b * tile, rank), bf16), pltpu.VMEM((LANES, rank), f32)],
            work, slab.size * 2, (meta, got, slab, a_bf3, c_bf),
        )
        got_c = swap(send, "col")
        mixed = got_c[:, slots * qa :]
        second = slots * depth + qb
        third = second + qb
        spots_k = mixed[:, 0, third + slots : third + 2 * slots]
        onehot = (spots_k[:, :, None] == lax.iota(jnp.int32, layers).astype(f32)).astype(f32)
        c_got = mixed[:, :, : slots * depth].reshape(nc, qa, slots, depth)
        drive_c = jnp.einsum("sqmk,smb->qbk", c_got, onehot, precision=HIGH).reshape(qa, length)
        strip = mixed[:, :, slots * depth : second].reshape(rank, qb)
        kept = LANES + qb
        strip = lax.dynamic_slice_in_dim(jnp.concatenate([strip, strip]), row * qb, kept, 0)
        place = lax.broadcasted_iota(jnp.int32, strip.shape, 0)
        strip = jnp.where((place < qb) | (place >= LANES), 0.5 * strip, strip).T
        rest = jnp.concatenate([strip[: qb // 2, LANES:], strip[qb // 2 :, LANES:]], axis=1)
        rest = jnp.pad(rest, [(0, qa - qb // 2), (0, 0)])
        piece_b = jnp.sum(mixed[:, :, second:third], axis=0)
        piece_b = pad_lanes(jnp.concatenate([piece_b, rest], axis=1))
        everyone = jnp.concatenate([strip[:, :LANES], fold(drive_c), piece_b], axis=0)
        everyone = jnp.broadcast_to(everyone[None], (nr,) + everyone.shape)
        got_r = swap(jnp.concatenate([blocks, everyone], axis=1), "row")
        last = sweep == sweeps - 1
        part_a, part_c = (tiles_a, qa, tile), (tiles_c, qa, LANES)
        shapes = [part_a, part_c] if last else [(nc // 2, (tiles_a + tiles_c) * qa, LANES)]
        results = call(
            functools.partial(project_kernel, sweep, last),
            shapes + [state_b.shape],
            [pltpu.VMEM((rank, rank), f32)],
            12 * rank * rank * tile, 8 * rank * rank * 4,
            (meta, step_sizes, got_c, got_r, at3, ct3, gram_c, state_b), scalars=2,
        )
        if last:
            new_a, new_c, state_b = results
        else:
            send, state_b = results
    per_a = tile // own_a
    own = new_a.reshape(tiles_a, qa, per_a, own_a).transpose(0, 2, 1, 3)
    own = own.reshape(nc // 2, 2, qa, own_a).swapaxes(1, 2).reshape(nc // 2, qa, 2 * own_a)
    own = fold(pad_lanes(own))
    everyone = jnp.broadcast_to(new_c.reshape(1, -1, LANES), (nc // 2, qa * tiles_c, LANES))
    got = chip_gather(jnp.concatenate([own, everyone], axis=1))
    a_got, c_got = take(got, [own.shape[1], qa * tiles_c])
    a_got = unfold(a_got, 2 * own_a + -2 * own_a % LANES)
    a_got = jnp.where(col % 2 == 0, a_got[:, :, :own_a], a_got[:, :, own_a : 2 * own_a])
    out_a = a_got.reshape(rank, own_a).T
    out_c = jnp.swapaxes(c_got.reshape(nc, tiles_c, qa, LANES), 0, 1).reshape(tiles_c, rank, LANES)
    out_c = jnp.swapaxes(out_c, 1, 2).reshape(length, rank)
    return out_a[None], state_b[None], out_c


def solution(mesh):
    placed = (
        P("row", "col", None, None, None, None),
        P("row", "col", None, None),
        P("row", "col"),
        P(),
        P("row", "col", None),
        P("col", "row", None),
        P(),
    )
    return jax.shard_map(
        shards,
        mesh=mesh,
        in_specs=placed,
        out_specs=(P("row", "col", None), P("col", "row", None), P()),
        check_vma=False,
    )
```
